128 devices in a mesh: scen: 32 (over y, x, z_lo), grp: 4 (over z_hi, core).
Axes of the slice: x: 4, y: 4, z: 4 (z_hi: 2, z_lo: 2; z = z_hi * 2 + z_lo), core: 2. Of those that a mesh axis runs over, the one named last changes fastest.
Arguments:
- coupling: bfloat16 [128, 768, 4096], P(('scen', 'grp')), may hold values from -6 to 6
- scen_kkt: bfloat16 [128, 768, 768], P(('scen', 'grp')), may hold values from -3 to 5, as said below
- active_rows: int32 [128], P(('scen', 'grp')), may hold values from 128 to 768, as said below
- first_hess: float32 [512], replicated, may hold values from 20 to 400
Outputs:
- factor_panels: float32 [4096, 512], P('scen')
The draws below stay inside these ranges and needn't reach their ends.
Inputs may be any that keep to these rules, and one draw needn't show every extreme that they name: `scen_kkt`: each block is symmetric positive definite: a Gram matrix of 768 columns divided by 768 plus a positive diagonal. `active_rows`: each count is a multiple of 128; some scenario has 768 and some has 128.
All inputs are finite; a program needn't handle non-finite values.
Results may differ from the reference program's by a relative error of at most 0.0011.
Values sent between devices are 32-bit elements; how exact they have to be, the bound alone decides.
A program may use at most 64 MiB of HBM per device.

```python
import math
import jax
import jax.numpy as jnp
from jax import lax

NB = 768
NC = 4096
PW = 256
TILE = 128
NSCEN = 128


def draw_scen_kkt(key, part):
    key_gram = jax.random.fold_in(key, 11)
    key_diag = jax.random.fold_in(key, 12)
    bound_value = math.sqrt(3.0)
    gram_src = jax.random.uniform(key_gram, (NSCEN, NB, NB), jnp.float32, -bound_value, bound_value)
    gram = jnp.einsum('sij,skj->sik', gram_src, gram_src) / NB
    offset_diag = jnp.exp(jax.random.uniform(key_diag, (NSCEN, NB), jnp.float32, math.log(0.02), math.log(0.5)))
    identity = jnp.eye(NB, dtype=jnp.float32)
    return (gram + offset_diag[:, :, None] * identity).astype(jnp.bfloat16)


def draw_active_rows(key, part):
    key_tiles = jax.random.fold_in(key, 21)
    key_order = jax.random.fold_in(key, 22)
    tiles = jax.random.randint(key_tiles, (NSCEN,), 1, NB // TILE + 1)
    order = jax.random.permutation(key_order, NSCEN)
    tiles = tiles.at[order[0]].set(NB // TILE)
    tiles = tiles.at[order[1]].set(1)
    return (tiles * TILE).astype(jnp.int32)


def raised(array, own_key, source, target, blocks, factor):
    owner, partner = [(jnp.arange(array.shape[position]) // (array.shape[position] // blocks)).reshape([-1 if axis == position else 1 for axis in range(array.ndim)]) for position in (source, target)]
    chosen = jax.random.permutation(own_key, blocks)[partner]
    strong = (owner == chosen) | (owner == (partner + blocks // 2) % blocks)
    return jnp.where(strong, factor * array, array)


def steps_of(stream_key, extent, pieces, least, high):
    gain = 1.0
    for dim, blocks in pieces:
        steps = jax.random.uniform(jax.random.fold_in(jax.random.fold_in(stream_key, 6), dim), (blocks,), jnp.float32, least / len(pieces), high / len(pieces))
        gain = gain * jnp.repeat(jnp.exp(steps), extent[dim] // blocks).reshape((-1,) + (1,) * (len(extent) - 1 - dim))
    return gain


def noise_with(key, shape, scale, reach, pieces, heavy, kind=jnp.bfloat16):
    drawn = scale * jax.random.normal(key, shape, jnp.float32)
    if pieces:
        drawn = drawn * steps_of(key, shape, pieces, -0.22, 0.18)
    return jnp.clip(raised(drawn, jax.random.fold_in(key, 3), *heavy), -reach, reach).astype(kind)


def setup_inputs(seed: int = 0) -> dict:
    key_of = jax.random.split(jax.random.key(seed), 5)
    return {
        "coupling": noise_with(key_of[0], (NSCEN, NB, NC), 0.25, 6.0, ((0, 128),), (0, 2, 128, 5.5)),
        "scen_kkt": draw_scen_kkt(jax.random.fold_in(key_of[4], 71), 0),
        "active_rows": draw_active_rows(jax.random.fold_in(key_of[4], 71), 0),
        "first_hess": jnp.clip(jnp.exp(jax.random.uniform(key_of[3], (2 * PW,), jnp.float32, math.log(20.0), math.log(400.0))), 20.0, 400.0),
    }


def solve_block(factor, right_side):
    return jax.scipy.linalg.cho_solve((factor, True), right_side)

def solve_right(lower_tri, rows):
    return jax.scipy.linalg.solve_triangular(lower_tri, rows.T, lower=True).T

def reference(coupling, scen_kkt, active_rows, first_hess):
    panel_cols = 2 * PW

    def add_scenario(running, scen_items):
        scen_block, kkt_block, active = scen_items
        keep_mask = (jnp.arange(NB, dtype=jnp.int32)[:, None] < active).astype(jnp.float32)
        coupling_panel = scen_block[:, :panel_cols].astype(jnp.float32) * keep_mask
        factor = jnp.linalg.cholesky(kkt_block.astype(jnp.float32))
        solved = (solve_block(factor, coupling_panel) * keep_mask).astype(jnp.bfloat16)
        term = jnp.dot(scen_block.astype(jnp.float32).T, solved.astype(jnp.float32), precision=lax.Precision.HIGHEST)
        return (running + term, None)
    start_panel = jnp.zeros((NC, panel_cols), jnp.float32)
    schur_panel, ignored = lax.scan(add_scenario, start_panel, (coupling, scen_kkt, active_rows))
    row_ids = jnp.arange(NC, dtype=jnp.int32)[:, None]
    col_ids = jnp.arange(panel_cols, dtype=jnp.int32)[None, :]
    schur_panel = schur_panel + jnp.where(row_ids == col_ids, first_hess[None, :], jnp.zeros((), jnp.float32))
    diag_one = jnp.linalg.cholesky(schur_panel[:PW, :PW])
    lower_one = solve_right(diag_one, schur_panel[PW:, :PW])
    updated = schur_panel[PW:, PW:] - jnp.dot(lower_one, lower_one[:PW].T, precision=lax.Precision.HIGHEST)
    diag_two = jnp.linalg.cholesky(updated[:PW])
    lower_two = solve_right(diag_two, updated[PW:])
    left_half = jnp.concatenate([diag_one, lower_one], 0)
    right_half = jnp.concatenate([jnp.zeros((PW, PW), jnp.float32), diag_two, lower_two], 0)
    return jnp.concatenate([left_half, right_half], 1)
```

```python
import jax
import jax.numpy as jnp
from jax import lax
from jax.experimental import pallas as pl
from jax.experimental.pallas import tpu as pltpu
from jax.sharding import PartitionSpec as P

PW = 256
NC = 4096
NB = 768
F32 = jnp.float32
HIGHEST = lax.Precision.HIGHEST
MESH = pl.DeviceIdType.MESH

ORDERS = (("x", "y", "z"), ("y", "z", "x"), ("z", "x", "y"))
MAIN_N = (5, 5, 6)
MAIN_OFF = (0, 5, 10)
TOP_N = (2, 2, 1)
TOP_OFF = (0, 32, 64)


def solve_block(factor, right_side):
    return jax.scipy.linalg.cho_solve((factor, True), right_side)


def solve_left(lower_tri, rows):
    return jax.scipy.linalg.solve_triangular(lower_tri, rows, lower=True)


def product_kernel(st_ref, c_ref, main_ref, top_ref, keep_ref):
    step = pl.program_id(0)
    y, x, zl = step // 8, (step // 2) % 4, step % 2
    res = jnp.dot(st_ref[...], c_ref[...], preferred_element_type=F32)
    for q in range(4):
        zh, c = q // 2, q % 2
        pos = {"x": x, "y": y, "z": 2 * zh + zl}
        for k in range(3):
            d0, d1, d2 = ORDERS[k]
            n = MAIN_N[k]
            idx = MAIN_OFF[k] * 64 + ((pos[d0] * 4 + pos[d1]) * 4 + pos[d2]) * n
            lo = q * 128 + MAIN_OFF[k] * 8
            main_ref[c, pl.ds(idx, n)] = res[lo : lo + 8 * n].reshape(n, 8, 128)

    @pl.when(step < 4)
    def _():
        keep_ref[step] = res

    @pl.when(step == 3)
    def _():
        def block(a, s):
            return keep_ref[s, a * 128 : (a + 1) * 128, :]

        def put(i, v):
            top_ref[i // 5, pl.ds((i % 5) * 16, 16)] = v.reshape(16, 8, 128)

        for base, (p, r) in ((0, (0, 1)), (7, (2, 3))):
            put(base, 0.5 * (block(p, p) + block(p, p).T))
            put(base + 1, 0.5 * (block(p, r) + block(r, p).T))
            put(base + 2, 0.5 * (block(r, r) + block(r, r).T))
        put(3, block(0, 2))
        put(4, block(1, 2))
        put(5, block(0, 3))
        put(6, block(1, 3))


def product(solved_t, coupling):
    return pl.pallas_call(
        product_kernel,
        grid=(32,),
        in_specs=[
            pl.BlockSpec((512, NB), lambda i: (0, 0)),
            pl.BlockSpec((NB, 128), lambda i: (0, i)),
        ],
        out_specs=[
            pl.BlockSpec((2, 1024, 8, 128), lambda i: (0, 0, 0, 0)),
            pl.BlockSpec((2, 80, 8, 128), lambda i: (0, 0, 0, 0)),
        ],
        out_shape=[
            jax.ShapeDtypeStruct((2, 1024, 8, 128), F32),
            jax.ShapeDtypeStruct((2, 80, 8, 128), F32),
        ],
        scratch_shapes=[pltpu.VMEM((4, 512, 128), F32)],
        compiler_params=pltpu.CompilerParams(vmem_limit_bytes=48 << 20),
    )(solved_t, coupling)


def exchange_kernel(
    main_ref, top_ref, own_ref, all_ref,
    acc, ra, r0, r1, r2, own, tacc, ta, t0, t1, t2, gat,
    core_s, core_r, st_s, st_r, tst_s, tst_r, ag_s, ag_r,
):
    si = lax.axis_index("scen")
    gi = lax.axis_index("grp")
    c = gi % 2
    zh = gi // 2
    pos = {"y": si // 8, "x": (si // 2) % 4, "z": 2 * zh + si % 2}

    def device(y, x, z, core):
        return {"scen": (y * 4 + x) * 2 + z % 2, "grp": (z // 2) * 2 + core}

    def peer(axis, dist):
        at = dict(pos)
        at[axis] = (at[axis] + dist) % 4
        return device(at["y"], at["x"], at["z"], c)

    partner = device(pos["y"], pos["x"], pos["z"], 1 - c)
    far = device(pos["y"], pos["x"], (pos["z"] + 2) % 4, 1 - c)

    barrier = pltpu.get_barrier_semaphore()
    greet = [peer(a, d) for a in "xyz" for d in (1, 2, 3)] + [partner, far]
    for dev in greet:
        pl.semaphore_signal(barrier, inc=1, device_id=dev, device_id_type=MESH)
    pl.semaphore_wait(barrier, len(greet))

    pending = []

    def send(src, dst, ssem, rsem, dev):
        cp = pltpu.make_async_remote_copy(
            src_ref=src, dst_ref=dst, send_sem=ssem, recv_sem=rsem,
            device_id=dev, device_id_type=MESH,
        )
        cp.start()
        pending.append(cp)
        return cp

    tcore = send(top_ref.at[1 - c], ta, core_s.at[0], core_r.at[0], partner)
    mcore = []
    for k in range(3):
        sl = pl.ds(MAIN_OFF[k] * 64, MAIN_N[k] * 64)
        mcore.append(
            send(main_ref.at[1 - c, sl], ra.at[sl], core_s.at[1 + k], core_r.at[1 + k], partner)
        )

    tcore.wait_recv()
    tacc[...] = top_ref[c] + ta[...]

    def scatter(buf, base, n, axis, slots, off, ssem, rsem, first):
        out = []
        for d in (1, 2, 3):
            p = (pos[axis] + d) % 4
            out.append(
                send(
                    buf.at[pl.ds(base + p * n, n)], slots.at[d - 1, pl.ds(off, n)],
                    ssem.at[first + d - 1], rsem.at[first + d - 1], peer(axis, d),
                )
            )
        return out

    def gather_sum(buf, base, n, slots, off, copies):
        for cp in copies:
            cp.wait_recv()
        own_piece = pl.ds(base, n)
        sl = pl.ds(off, n)
        buf[own_piece] = buf[own_piece] + slots[0, sl] + slots[1, sl] + slots[2, sl]

    base = list(TOP_OFF)
    for stage, slots in ((0, t0), (1, t1)):
        flights = []
        for k in range(3):
            n = TOP_N[k] * (4 if stage == 0 else 1)
            off = TOP_OFF[k] // 4 if stage == 0 else TOP_OFF[k] // 16
            axis = ORDERS[k][stage]
            flights.append(
                scatter(tacc, base[k], n, axis, slots, off, tst_s, tst_r, (stage * 3 + k) * 3)
            )
        for k in range(3):
            n = TOP_N[k] * (4 if stage == 0 else 1)
            off = TOP_OFF[k] // 4 if stage == 0 else TOP_OFF[k] // 16
            base[k] = base[k] + pos[ORDERS[k][stage]] * n
            gather_sum(tacc, base[k], n, slots, off, flights[k])
    flights = []
    for k in range(3):
        n, off = TOP_N[k], TOP_OFF[k] // 16
        axis = ORDERS[k][2]
        flights.append([
            send(
                tacc.at[pl.ds(base[k], n)], t2.at[d - 1, pl.ds(off, n)],
                tst_s.at[(6 + k) * 3 + d - 1], tst_r.at[(6 + k) * 3 + d - 1], peer(axis, d),
            )
            for d in (1, 2, 3)
        ])
    for k in range(3):
        n, off = TOP_N[k], TOP_OFF[k] // 16
        for cp in flights[k]:
            cp.wait_recv()
        mine = pos[ORDERS[k][2]]
        parts = [tacc[pl.ds(base[k], n)]] + [t2[d, pl.ds(off, n)] for d in range(3)]
        total = None
        for p in range(4):
            dist = (mine - p) % 4
            v = jnp.where(
                dist == 0, parts[0],
                jnp.where(dist == 1, parts[1], jnp.where(dist == 2, parts[2], parts[3])),
            )
            total = v if total is None else total + v
        gat[c, pl.ds(base[k], n)] = total
    for stage in (1, 0):
        flights = []
        for k in range(3):
            n = TOP_N[k] * (1 if stage == 1 else 4)
            if stage == 0:
                base[k] = base[k] - pos[ORDERS[k][1]] * TOP_N[k]
            piece = gat.at[c, pl.ds(base[k], n)]
            first = ((1 - stage) * 3 + k) * 3
            flights.append([
                send(piece, piece, ag_s.at[first + d - 1], ag_r.at[first + d - 1],
                     peer(ORDERS[k][stage], d))
                for d in (1, 2, 3)
            ])
        for k in range(3):
            for cp in flights[k]:
                cp.wait_recv()
    last = send(gat.at[c], gat.at[c], ag_s.at[18], ag_r.at[18], partner)

    base = [MAIN_OFF[k] * 64 for k in range(3)]
    flights = []
    for k in range(3):
        mcore[k].wait_recv()
        sl = pl.ds(MAIN_OFF[k] * 64, MAIN_N[k] * 64)
        acc[sl] = main_ref[c, sl] + ra[sl]
        flights.append(
            scatter(acc, base[k], 16 * MAIN_N[k], ORDERS[k][0], r0, MAIN_OFF[k] * 16,
                    st_s, st_r, k * 3)
        )
    for stage, slots, m in ((0, r0, 16), (1, r1, 4), (2, r2, 1)):
        following = []
        for k in range(3):
            n = MAIN_N[k] * m
            base[k] = base[k] + pos[ORDERS[k][stage]] * n
            gather_sum(acc, base[k], n, slots, MAIN_OFF[k] * m, flights[k])
            if stage < 2:
                following.append(
                    scatter(acc, base[k], n // 4, ORDERS[k][stage + 1], (r1, r2)[stage],
                            MAIN_OFF[k] * (m // 4), st_s, st_r, ((stage + 1) * 3 + k) * 3)
                )
        flights = following
    for k in range(3):
        own[gi, pl.ds(MAIN_OFF[k], MAIN_N[k])] = acc[pl.ds(base[k], MAIN_N[k])]
    mine = own.at[gi]
    flights = [
        send(mine, mine, ag_s.at[19 + j], ag_r.at[19 + j], dev)
        for j, dev in enumerate((partner, peer("z", 2), far))
    ]
    for cp in flights:
        cp.wait_recv()
    own_ref[...] = own[...]
    last.wait_recv()
    all_ref[...] = gat[...]
    for cp in pending:
        cp.wait_send()


def exchange(main, top):
    tile = (8, 128)
    vm = lambda *lead: pltpu.VMEM(lead + tile, F32)
    sem = lambda n: pltpu.SemaphoreType.DMA((n,))
    vspec = pl.BlockSpec(memory_space=pltpu.VMEM)
    return pl.pallas_call(
        exchange_kernel,
        in_specs=[vspec, vspec],
        out_specs=[vspec, vspec],
        out_shape=[
            jax.ShapeDtypeStruct((4, 16) + tile, F32),
            jax.ShapeDtypeStruct((2, 80) + tile, F32),
        ],
        scratch_shapes=[
            vm(1024), vm(1024), vm(3, 256), vm(3, 64), vm(3, 16), vm(4, 16),
            vm(80), vm(80), vm(3, 20), vm(3, 5), vm(3, 5), vm(2, 80),
            sem(4), sem(4), sem(27), sem(27), sem(27), sem(27), sem(22), sem(22),
        ],
        compiler_params=pltpu.CompilerParams(
            collective_id=0, has_side_effects=True, vmem_limit_bytes=48 << 20
        ),
    )(main, top)


def per_device(coupling, scen_kkt, active_rows, first_hess):
    si = lax.axis_index("scen")
    tile_pos = lax.broadcasted_iota(jnp.int32, (1, NB, 1), 1)
    keep_mask = (tile_pos < active_rows[:, None, None]).astype(F32)
    coupling_panel = coupling[:, :, : 2 * PW].astype(F32) * keep_mask
    factor = jnp.linalg.cholesky(scen_kkt.astype(F32))
    solved = (jax.vmap(solve_block)(factor, coupling_panel) * keep_mask).astype(jnp.bfloat16)
    main, top = product(solved[0].T, coupling[0])
    own, gathered = exchange(main, top)
    own_t = own.reshape(512, 128)
    b = gathered.reshape(10, 128, 128)
    d1 = jnp.block([[b[0], b[1]], [b[1].T, b[2]]]) + jnp.diag(first_hess[:PW])
    d2 = jnp.block([[b[7], b[8]], [b[8].T, b[9]]]) + jnp.diag(first_hess[PW:])
    m21 = jnp.block([[b[3], b[5]], [b[4], b[6]]])
    row = si * 128 + lax.broadcasted_iota(jnp.int32, (1, 128), 1)
    col = lax.broadcasted_iota(jnp.int32, (512, 1), 0)
    own_t = own_t + jnp.where(row == col, first_hess[:, None], 0.0)
    diag_one = jnp.linalg.cholesky(d1, symmetrize_input=False)
    y1 = solve_left(diag_one, jnp.concatenate([m21, own_t[:PW]], 1))
    mid_t, y1 = y1[:, :PW], y1[:, PW:]
    upd = d2 - jnp.dot(mid_t.T, mid_t, precision=HIGHEST)
    diag_two = jnp.linalg.cholesky(upd)
    y2 = own_t[PW:] - jnp.dot(mid_t.T, y1, precision=HIGHEST)
    y2 = solve_left(diag_two, y2)
    out = jnp.concatenate([y1, y2], 0).T
    top_factor = jnp.block([[diag_one, jnp.zeros((PW, PW), F32)], [mid_t.T, diag_two]])
    take = lax.dynamic_slice_in_dim(top_factor, jnp.minimum(si, 3) * 128, 128, 0)
    return jnp.where(si < 4, take, out)


def solution(mesh):
    placed = (
        P(("scen", "grp"), None, None),
        P(("scen", "grp"), None, None),
        P(("scen", "grp")),
        P(),
    )
    return jax.shard_map(
        per_device, mesh=mesh, in_specs=placed, out_specs=P("scen", None), check_vma=False
    )
```

```python
import jax
import jax.numpy as jnp
from jax import lax
from jax.experimental import pallas as pl
from jax.experimental.pallas import tpu as pltpu
from jax.sharding import PartitionSpec as P

PW = 256
NC = 4096
NB = 768
F32 = jnp.float32
HIGHEST = lax.Precision.HIGHEST
MESH = pl.DeviceIdType.MESH

ORDERS = (("x", "y", "z"), ("y", "z", "x"), ("z", "x", "y"))
MAIN_N = (5, 5, 6)
MAIN_OFF = (0, 5, 10)
TOP_N = (2, 2, 1)
TOP_OFF = (0, 32, 64)


def total(terms):
    while len(terms) > 1:
        terms = [terms[i] + terms[i + 1] if i + 1 < len(terms) else terms[i] for i in range(0, len(terms), 2)]
    return terms[0]

def inverse_factor(z):
    shape = (8, 128)
    lane = lax.broadcasted_iota(jnp.int32, shape, 1)
    sub = lax.broadcasted_iota(jnp.int32, shape, 0)
    z = list(z)
    for j in range(16):
        lo = 8 * j
        zj = z[j]
        col = [jnp.broadcast_to(zj[:, lo + c : lo + c + 1], shape) for c in range(8)]
        e = {(r, c): jnp.broadcast_to(col[c][r : r + 1], shape) for c in range(8) for r in range(c, 8)}
        inv, l, t = {}, {}, {}
        for c in range(8):
            inv[c] = lax.rsqrt(e[c, c])
            for r in range(c + 1, 8):
                l[r, c] = e[r, c] * inv[c]
            for r in range(c + 1, 8):
                for q in range(c + 1, r + 1):
                    e[r, q] = e[r, q] - l[r, c] * l[q, c]
        for c in range(8):
            t[c, c] = inv[c]
            for r in range(c + 1, 8):
                t[r, c] = -inv[r] * total([l[r, m] * t[m, c] for m in range(c, r)])
        panel = (lane >= lo) & (lane < lo + 8)
        zp = jnp.where(panel, jnp.where(lane - lo == sub, 1.0, 0.0), zj)
        zb = [jnp.broadcast_to(zp[c : c + 1], shape) for c in range(8)]
        u = [total([t[r, c] * zb[c] for c in range(r + 1)]) for r in range(8)]
        w = [total([t[c, r] * u[c] for c in range(r, 8)]) for r in range(8)]
        row = u[0]
        for r in range(1, 8):
            row = jnp.where(sub == r, u[r], row)
        z[j] = jnp.where(lane < lo + 8, row, 0.0)
        for i in range(j + 1, 16):
            zi = z[i]
            q = [jnp.broadcast_to(zi[:, lo + c : lo + c + 1], shape) * w[c] for c in range(8)]
            z[i] = jnp.where(panel, 0.0, zi) - total(q)
    return z

def dot(a, b):
    return jnp.dot(a, b, precision=HIGHEST, preferred_element_type=F32)

def dot_t(a, b):
    return lax.dot_general(a, b, (((0,), (0,)), ((), ())), precision=HIGHEST, preferred_element_type=F32)

def solve_kernel(act_ref, k_ref, c_ref, st_ref, aug, linv, xs):
    row = lax.broadcasted_iota(jnp.int32, (NB, 1), 0)
    keep = (row < act_ref[0]).astype(F32)
    aug[:, :NB] = k_ref[...].astype(F32)
    aug[:, NB:] = c_ref[...].astype(F32) * keep

    def step(j, _):
        at = pl.multiple_of(j * 128, 128)
        rows = pl.ds(at, 128)
        z = [aug[pl.ds(at + 8 * i, 8), pl.ds(at, 128)] for i in range(16)]
        z = inverse_factor(z)
        for i in range(16):
            linv[j, 8 * i : 8 * i + 8, :] = z[i]
        y = dot(linv[j], aug[rows, :])
        aug[rows, :] = y

        def update(i, _):
            ai = pl.multiple_of(i * 128, 128)
            g = aug[rows, pl.ds(ai, 128)]
            below = pl.ds(ai, 128)
            aug[below, :] = aug[below, :] - dot_t(g, aug[rows, :])
            return 0

        lax.fori_loop(j + 1, NB // 128, update, 0)
        return 0

    lax.fori_loop(0, NB // 128, step, 0)
    for j in range(NB // 128 - 1, -1, -1):
        lo, hi = j * 128, j * 128 + 128
        acc = aug[lo:hi, NB:]
        if hi < NB:
            acc = acc - dot(aug[lo:hi, hi:NB], xs[hi:, :])
        x = dot_t(linv[j], acc)
        xs[lo:hi, :] = x
        st_ref[:, lo:hi] = (x * keep[lo:hi]).T.astype(jnp.bfloat16)

def scenario_solve(active, kkt, coupling):
    vspec = pl.BlockSpec(memory_space=pltpu.VMEM)
    return pl.pallas_call(
        solve_kernel,
        grid=(1,),
        in_specs=[pl.BlockSpec(memory_space=pltpu.SMEM), pl.BlockSpec((NB, NB), lambda i: (0, 0)),
                  pl.BlockSpec((NB, 512), lambda i: (0, 0))],
        out_specs=pl.BlockSpec((512, NB), lambda i: (0, 0)),
        out_shape=jax.ShapeDtypeStruct((512, NB), jnp.bfloat16),
        scratch_shapes=[pltpu.VMEM((NB, 1280), F32), pltpu.VMEM((6, 128, 128), F32), pltpu.VMEM((NB, 512), F32)],
        compiler_params=pltpu.CompilerParams(vmem_limit_bytes=48 << 20),
    )(active, kkt, coupling)


def product_kernel(st_ref, c_ref, main_ref, top_ref, keep_ref):
    step = pl.program_id(0)
    res = jnp.dot(st_ref[...], c_ref[...], preferred_element_type=F32)
    for t in range(4):
        y, x, zl = step // 2, (step % 2) * 2 + t // 2, t % 2
        part = res[:, t * 128 : (t + 1) * 128]
        for q in range(4):
            zh, c = q // 2, q % 2
            pos = {"x": x, "y": y, "z": 2 * zh + zl}
            for k in range(3):
                d0, d1, d2 = ORDERS[k]
                n = MAIN_N[k]
                idx = MAIN_OFF[k] * 64 + ((pos[d0] * 4 + pos[d1]) * 4 + pos[d2]) * n
                lo = q * 128 + MAIN_OFF[k] * 8
                main_ref[c, pl.ds(idx, n)] = part[lo : lo + 8 * n].reshape(n, 8, 128)

    @pl.when(step == 0)
    def _():
        keep_ref[...] = res

        def block(a, s):
            return keep_ref[a * 128 : (a + 1) * 128, s * 128 : (s + 1) * 128]

        def put(i, v):
            top_ref[i // 5, pl.ds((i % 5) * 16, 16)] = v.reshape(16, 8, 128)

        for base, (p, r) in ((0, (0, 1)), (7, (2, 3))):
            put(base, 0.5 * (block(p, p) + block(p, p).T))
            put(base + 1, 0.5 * (block(p, r) + block(r, p).T))
            put(base + 2, 0.5 * (block(r, r) + block(r, r).T))
        put(3, block(0, 2))
        put(4, block(1, 2))
        put(5, block(0, 3))
        put(6, block(1, 3))


def product(solved_t, coupling):
    return pl.pallas_call(
        product_kernel,
        grid=(8,),
        in_specs=[
            pl.BlockSpec((512, NB), lambda i: (0, 0)),
            pl.BlockSpec((NB, 512), lambda i: (0, i)),
        ],
        out_specs=[
            pl.BlockSpec((2, 1024, 8, 128), lambda i: (0, 0, 0, 0)),
            pl.BlockSpec((2, 80, 8, 128), lambda i: (0, 0, 0, 0)),
        ],
        out_shape=[
            jax.ShapeDtypeStruct((2, 1024, 8, 128), F32),
            jax.ShapeDtypeStruct((2, 80, 8, 128), F32),
        ],
        scratch_shapes=[pltpu.VMEM((512, 512), F32)],
        compiler_params=pltpu.CompilerParams(vmem_limit_bytes=48 << 20),
    )(solved_t, coupling)


def exchange_kernel(
    main_ref, top_ref, own_ref, all_ref,
    acc, ra, r0, r1, r2, own, tacc, ta, t0, t1, t2, gat,
    core_s, core_r, st_s, st_r, tst_s, tst_r, ag_s, ag_r,
):
    si = lax.axis_index("scen")
    gi = lax.axis_index("grp")
    c = gi % 2
    zh = gi // 2
    pos = {"y": si // 8, "x": (si // 2) % 4, "z": 2 * zh + si % 2}

    def device(y, x, z, core):
        return {"scen": (y * 4 + x) * 2 + z % 2, "grp": (z // 2) * 2 + core}

    def peer(axis, dist):
        at = dict(pos)
        at[axis] = (at[axis] + dist) % 4
        return device(at["y"], at["x"], at["z"], c)

    partner = device(pos["y"], pos["x"], pos["z"], 1 - c)
    far = device(pos["y"], pos["x"], (pos["z"] + 2) % 4, 1 - c)

    barrier = pltpu.get_barrier_semaphore()
    greet = [peer(a, d) for a in "xyz" for d in (1, 2, 3)] + [partner, far]
    for dev in greet:
        pl.semaphore_signal(barrier, inc=1, device_id=dev, device_id_type=MESH)
    pl.semaphore_wait(barrier, len(greet))

    pending = []

    def send(src, dst, ssem, rsem, dev):
        cp = pltpu.make_async_remote_copy(
            src_ref=src, dst_ref=dst, send_sem=ssem, recv_sem=rsem,
            device_id=dev, device_id_type=MESH,
        )
        cp.start()
        pending.append(cp)
        return cp

    tcore = send(top_ref.at[1 - c], ta, core_s.at[0], core_r.at[0], partner)
    mcore = []
    for k in range(3):
        sl = pl.ds(MAIN_OFF[k] * 64, MAIN_N[k] * 64)
        mcore.append(
            send(main_ref.at[1 - c, sl], ra.at[sl], core_s.at[1 + k], core_r.at[1 + k], partner)
        )

    tcore.wait_recv()
    tacc[...] = top_ref[c] + ta[...]

    def scatter(buf, base, n, axis, slots, off, ssem, rsem, first):
        out = []
        for d in (1, 2, 3):
            p = (pos[axis] + d) % 4
            out.append(
                send(
                    buf.at[pl.ds(base + p * n, n)], slots.at[d - 1, pl.ds(off, n)],
                    ssem.at[first + d - 1], rsem.at[first + d - 1], peer(axis, d),
                )
            )
        return out

    def gather_sum(buf, base, n, slots, off, copies):
        for cp in copies:
            cp.wait_recv()
        own_piece = pl.ds(base, n)
        sl = pl.ds(off, n)
        buf[own_piece] = buf[own_piece] + slots[0, sl] + slots[1, sl] + slots[2, sl]

    base = list(TOP_OFF)
    for stage, slots in ((0, t0), (1, t1)):
        flights = []
        for k in range(3):
            n = TOP_N[k] * (4 if stage == 0 else 1)
            off = TOP_OFF[k] // 4 if stage == 0 else TOP_OFF[k] // 16
            axis = ORDERS[k][stage]
            flights.append(
                scatter(tacc, base[k], n, axis, slots, off, tst_s, tst_r, (stage * 3 + k) * 3)
            )
        for k in range(3):
            n = TOP_N[k] * (4 if stage == 0 else 1)
            off = TOP_OFF[k] // 4 if stage == 0 else TOP_OFF[k] // 16
            base[k] = base[k] + pos[ORDERS[k][stage]] * n
            gather_sum(tacc, base[k], n, slots, off, flights[k])
    flights = []
    for k in range(3):
        n, off = TOP_N[k], TOP_OFF[k] // 16
        axis = ORDERS[k][2]
        flights.append([
            send(
                tacc.at[pl.ds(base[k], n)], t2.at[d - 1, pl.ds(off, n)],
                tst_s.at[(6 + k) * 3 + d - 1], tst_r.at[(6 + k) * 3 + d - 1], peer(axis, d),
            )
            for d in (1, 2, 3)
        ])
    for k in range(3):
        n, off = TOP_N[k], TOP_OFF[k] // 16
        for cp in flights[k]:
            cp.wait_recv()
        mine = pos[ORDERS[k][2]]
        parts = [tacc[pl.ds(base[k], n)]] + [t2[d, pl.ds(off, n)] for d in range(3)]
        total = None
        for p in range(4):
            dist = (mine - p) % 4
            v = jnp.where(
                dist == 0, parts[0],
                jnp.where(dist == 1, parts[1], jnp.where(dist == 2, parts[2], parts[3])),
            )
            total = v if total is None else total + v
        gat[c, pl.ds(base[k], n)] = total
    for stage in (1, 0):
        flights = []
        for k in range(3):
            n = TOP_N[k] * (1 if stage == 1 else 4)
            if stage == 0:
                base[k] = base[k] - pos[ORDERS[k][1]] * TOP_N[k]
            piece = gat.at[c, pl.ds(base[k], n)]
            first = ((1 - stage) * 3 + k) * 3
            flights.append([
                send(piece, piece, ag_s.at[first + d - 1], ag_r.at[first + d - 1],
                     peer(ORDERS[k][stage], d))
                for d in (1, 2, 3)
            ])
        for k in range(3):
            for cp in flights[k]:
                cp.wait_recv()
    last = send(gat.at[c], gat.at[c], ag_s.at[18], ag_r.at[18], partner)

    base = [MAIN_OFF[k] * 64 for k in range(3)]
    flights = []
    for k in range(3):
        mcore[k].wait_recv()
        sl = pl.ds(MAIN_OFF[k] * 64, MAIN_N[k] * 64)
        acc[sl] = main_ref[c, sl] + ra[sl]
        flights.append(
            scatter(acc, base[k], 16 * MAIN_N[k], ORDERS[k][0], r0, MAIN_OFF[k] * 16,
                    st_s, st_r, k * 3)
        )
    for stage, slots, m in ((0, r0, 16), (1, r1, 4), (2, r2, 1)):
        following = []
        for k in range(3):
            n = MAIN_N[k] * m
            base[k] = base[k] + pos[ORDERS[k][stage]] * n
            gather_sum(acc, base[k], n, slots, MAIN_OFF[k] * m, flights[k])
            if stage < 2:
                following.append(
                    scatter(acc, base[k], n // 4, ORDERS[k][stage + 1], (r1, r2)[stage],
                            MAIN_OFF[k] * (m // 4), st_s, st_r, ((stage + 1) * 3 + k) * 3)
                )
        flights = following
    for k in range(3):
        own[gi, pl.ds(MAIN_OFF[k], MAIN_N[k])] = acc[pl.ds(base[k], MAIN_N[k])]
    mine = own.at[gi]
    flights = [
        send(mine, mine, ag_s.at[19 + j], ag_r.at[19 + j], dev)
        for j, dev in enumerate((partner, peer("z", 2), far))
    ]
    for cp in flights:
        cp.wait_recv()
    own_ref[...] = own[...]
    last.wait_recv()
    all_ref[...] = gat[...]
    for cp in pending:
        cp.wait_send()


def exchange(main, top):
    tile = (8, 128)
    vm = lambda *lead: pltpu.VMEM(lead + tile, F32)
    sem = lambda n: pltpu.SemaphoreType.DMA((n,))
    vspec = pl.BlockSpec(memory_space=pltpu.VMEM)
    return pl.pallas_call(
        exchange_kernel,
        in_specs=[vspec, vspec],
        out_specs=[vspec, vspec],
        out_shape=[
            jax.ShapeDtypeStruct((4, 16) + tile, F32),
            jax.ShapeDtypeStruct((2, 80) + tile, F32),
        ],
        scratch_shapes=[
            vm(1024), vm(1024), vm(3, 256), vm(3, 64), vm(3, 16), vm(4, 16),
            vm(80), vm(80), vm(3, 20), vm(3, 5), vm(3, 5), vm(2, 80),
            sem(4), sem(4), sem(27), sem(27), sem(27), sem(27), sem(22), sem(22),
        ],
        compiler_params=pltpu.CompilerParams(
            collective_id=0, has_side_effects=True, vmem_limit_bytes=48 << 20
        ),
    )(main, top)


UPPER = ((0, 0), (0, 1), (1, 1), (0, 2), (1, 2), (0, 3), (1, 3), (2, 2), (2, 3), (3, 3))


def panel_kernel(hess_ref, own_ref, all_ref, out_ref, aug, linv):
    si = lax.axis_index("scen")
    row = lax.broadcasted_iota(jnp.int32, (128, 128), 0)
    lane = lax.broadcasted_iota(jnp.int32, (128, 128), 1)
    for i, (a, b) in enumerate(UPPER):
        v = all_ref[i // 5, pl.ds((i % 5) * 16, 16)].reshape(128, 128)
        if a == b:
            v = v + jnp.where(row == lane, hess_ref[a : a + 1, :], 0.0)
        aug[a * 128 : (a + 1) * 128, b * 128 : (b + 1) * 128] = v
    aug[:, 512:] = own_ref[...].reshape(512, 128)

    def step(j, _):
        at = pl.multiple_of(j * 128, 128)
        rows = pl.ds(at, 128)
        z = [aug[pl.ds(at + 8 * i, 8), pl.ds(at, 128)] for i in range(16)]
        z = inverse_factor(z)
        for i in range(16):
            linv[8 * i : 8 * i + 8, :] = z[i]
        aug[rows, :] = dot(linv[...], aug[rows, :])

        def update(i, _):
            ai = pl.multiple_of(i * 128, 128)
            below = pl.ds(ai, 128)
            aug[below, :] = aug[below, :] - dot_t(aug[rows, pl.ds(ai, 128)], aug[rows, :])
            return 0

        lax.fori_loop(j + 1, 4, update, 0)
        return 0

    lax.fori_loop(0, 4, step, 0)
    at = pl.multiple_of(jnp.where(si < 4, si, 4) * 128, 128)
    for j in range(4):
        v = aug[j * 128 : (j + 1) * 128, pl.ds(at, 128)]
        v = jnp.where(j * 128 + row <= si * 128 + lane, v, 0.0)
        out_ref[:, j * 128 : (j + 1) * 128] = v.T


def panel(hess, own, gathered):
    vspec = pl.BlockSpec(memory_space=pltpu.VMEM)
    return pl.pallas_call(
        panel_kernel,
        in_specs=[vspec, vspec, vspec],
        out_specs=vspec,
        out_shape=jax.ShapeDtypeStruct((128, 512), F32),
        scratch_shapes=[pltpu.VMEM((512, 640), F32), pltpu.VMEM((128, 128), F32)],
        compiler_params=pltpu.CompilerParams(vmem_limit_bytes=16 << 20),
    )(hess, own, gathered)


def per_device(coupling, scen_kkt, active_rows, first_hess):
    solved_t = scenario_solve(active_rows, scen_kkt[0], coupling[0])
    main, top = product(solved_t, coupling[0])
    own, gathered = exchange(main, top)
    return panel(first_hess.reshape(4, 128), own, gathered)


def solution(mesh):
    placed = (
        P(("scen", "grp"), None, None),
        P(("scen", "grp"), None, None),
        P(("scen", "grp")),
        P(),
    )
    return jax.shard_map(
        per_device, mesh=mesh, in_specs=placed, out_specs=P("scen", None), check_vma=False
    )
```

```python
import jax
import jax.numpy as jnp
from jax import lax
from jax.experimental import pallas as pl
from jax.experimental.pallas import tpu as pltpu
from jax.sharding import PartitionSpec as P

PW = 256
NC = 4096
NB = 768
F32 = jnp.float32
HIGHEST = lax.Precision.HIGHEST
MESH = pl.DeviceIdType.MESH

ORDERS = (("x", "y", "z"), ("y", "z", "x"), ("z", "x", "y"))
MAIN_N = (5, 5, 6)
MAIN_OFF = (0, 5, 10)
TOP_N = (2, 2, 1)
TOP_OFF = (0, 32, 64)


def total(terms):
    while len(terms) > 1:
        terms = [terms[i] + terms[i + 1] if i + 1 < len(terms) else terms[i] for i in range(0, len(terms), 2)]
    return terms[0]

def inverse_factor(z):
    shape = (8, 128)
    lane = lax.broadcasted_iota(jnp.int32, shape, 1)
    sub = lax.broadcasted_iota(jnp.int32, shape, 0)
    z = list(z)
    for j in range(16):
        lo = 8 * j
        zj = z[j]
        col = [jnp.broadcast_to(zj[:, lo + c : lo + c + 1], shape) for c in range(8)]
        e = {(r, c): jnp.broadcast_to(col[c][r : r + 1], shape) for c in range(8) for r in range(c, 8)}
        inv, l, t = {}, {}, {}
        for c in range(8):
            inv[c] = lax.rsqrt(e[c, c])
            for r in range(c + 1, 8):
                l[r, c] = e[r, c] * inv[c]
            for r in range(c + 1, 8):
                for q in range(c + 1, r + 1):
                    e[r, q] = e[r, q] - l[r, c] * l[q, c]
        for c in range(8):
            t[c, c] = inv[c]
            for r in range(c + 1, 8):
                t[r, c] = -inv[r] * total([l[r, m] * t[m, c] for m in range(c, r)])
        panel = (lane >= lo) & (lane < lo + 8)
        zp = jnp.where(panel, jnp.where(lane - lo == sub, 1.0, 0.0), zj)
        zb = [jnp.broadcast_to(zp[c : c + 1], shape) for c in range(8)]
        u = [total([t[r, c] * zb[c] for c in range(r + 1)]) for r in range(8)]
        w = [total([t[c, r] * u[c] for c in range(r, 8)]) for r in range(8)]
        row = u[0]
        for r in range(1, 8):
            row = jnp.where(sub == r, u[r], row)
        z[j] = jnp.where(lane < lo + 8, row, 0.0)
        for i in range(j + 1, 16):
            zi = z[i]
            q = [jnp.broadcast_to(zi[:, lo + c : lo + c + 1], shape) * w[c] for c in range(8)]
            z[i] = jnp.where(panel, 0.0, zi) - total(q)
    return z

def dot(a, b):
    return jnp.dot(a, b, precision=HIGHEST, preferred_element_type=F32)

def dot_t(a, b):
    return lax.dot_general(a, b, (((0,), (0,)), ((), ())), precision=HIGHEST, preferred_element_type=F32)

def solve_kernel(act_ref, k_ref, c_ref, st_ref, aug, linv, xs):
    row = lax.broadcasted_iota(jnp.int32, (NB, 1), 0)
    keep = (row < act_ref[0]).astype(F32)
    aug[:, :NB] = k_ref[...].astype(F32)
    aug[:, NB:] = c_ref[...].astype(F32) * keep

    def step(j, _):
        at = pl.multiple_of(j * 128, 128)
        rows = pl.ds(at, 128)
        z = [aug[pl.ds(at + 8 * i, 8), pl.ds(at, 128)] for i in range(16)]
        z = inverse_factor(z)
        for i in range(16):
            linv[j, 8 * i : 8 * i + 8, :] = z[i]
        y = dot(linv[j], aug[rows, :])
        aug[rows, :] = y

        def update(i, _):
            ai = pl.multiple_of(i * 128, 128)
            g = aug[rows, pl.ds(ai, 128)]
            below = pl.ds(ai, 128)
            aug[below, :] = aug[below, :] - dot_t(g, aug[rows, :])
            return 0

        lax.fori_loop(j + 1, NB // 128, update, 0)
        return 0

    lax.fori_loop(0, NB // 128, step, 0)
    for j in range(NB // 128 - 1, -1, -1):
        lo, hi = j * 128, j * 128 + 128
        acc = aug[lo:hi, NB:]
        if hi < NB:
            acc = acc - dot(aug[lo:hi, hi:NB], xs[hi:, :])
        x = dot_t(linv[j], acc)
        xs[lo:hi, :] = x
        st_ref[:, lo:hi] = (x * keep[lo:hi]).T.astype(jnp.bfloat16)

def scenario_solve(active, kkt, coupling):
    vspec = pl.BlockSpec(memory_space=pltpu.VMEM)
    return pl.pallas_call(
        solve_kernel,
        grid=(1,),
        in_specs=[pl.BlockSpec(memory_space=pltpu.SMEM), pl.BlockSpec((NB, NB), lambda i: (0, 0)),
                  pl.BlockSpec((NB, 512), lambda i: (0, 0))],
        out_specs=pl.BlockSpec((512, NB), lambda i: (0, 0)),
        out_shape=jax.ShapeDtypeStruct((512, NB), jnp.bfloat16),
        scratch_shapes=[pltpu.VMEM((NB, 1280), F32), pltpu.VMEM((6, 128, 128), F32), pltpu.VMEM((NB, 512), F32)],
        compiler_params=pltpu.CompilerParams(vmem_limit_bytes=48 << 20),
    )(active, kkt, coupling)


UPPER = ((0, 0), (0, 1), (1, 1), (0, 2), (1, 2), (0, 3), (1, 3), (2, 2), (2, 3), (3, 3))


def tail_kernel(
    hess_ref, st_ref, coup_ref, out_ref,
    cbuf, ma, mb, mc, ra, rb, rc, pa, pb, pc, qa, qb, qc, last_slots, own,
    keep, top, tacc, ta, t0, t1, t2, gat, aug, linv,
    c_sem, core_s, core_r, tcore_s, tcore_r, st_s, st_r, tst_s, tst_r, ag_s, ag_r,
):
    si = lax.axis_index("scen")
    gi = lax.axis_index("grp")
    c = gi % 2
    zh = gi // 2
    pos = {"y": si // 8, "x": (si // 2) % 4, "z": 2 * zh + si % 2}
    main, recv_core = (ma, mb, mc), (ra, rb, rc)
    slots = ((pa, pb, pc), (qa, qb, qc))

    loads = [
        pltpu.make_async_copy(coup_ref.at[:, pl.ds(i * 512, 512)], cbuf.at[i], c_sem.at[i])
        for i in range(8)
    ]
    for cp in loads:
        cp.start()

    def device(y, x, z, core):
        return {"scen": (y * 4 + x) * 2 + z % 2, "grp": (z // 2) * 2 + core}

    def peer(axis, dist):
        at = dict(pos)
        at[axis] = (at[axis] + dist) % 4
        return device(at["y"], at["x"], at["z"], c)

    partner = device(pos["y"], pos["x"], pos["z"], 1 - c)
    far = device(pos["y"], pos["x"], (pos["z"] + 2) % 4, 1 - c)

    barrier = pltpu.get_barrier_semaphore()
    greet = [peer(a, d) for a in "xyz" for d in (1, 2, 3)] + [partner, far]
    for dev in greet:
        pl.semaphore_signal(barrier, inc=1, device_id=dev, device_id_type=MESH)
    pl.semaphore_wait(barrier, len(greet))

    pending = []

    def send(src, dst, ssem, rsem, dev):
        cp = pltpu.make_async_remote_copy(
            src_ref=src, dst_ref=dst, send_sem=ssem, recv_sem=rsem,
            device_id=dev, device_id_type=MESH,
        )
        cp.start()
        pending.append(cp)
        return cp

    chunk_flights = []

    def region(k, y, x0):
        at = {"x": pl.ds(x0, 2), "y": y, "z": pl.ds(0, 4)}
        return tuple(at[a] for a in ORDERS[k])

    def chunk(i):
        y, x0 = i // 2, (i % 2) * 2
        loads[i].wait()
        res = jnp.dot(st_ref[...], cbuf[i], preferred_element_type=F32)
        if i == 0:
            keep[...] = res
        for t in range(4):
            x, zl = x0 + t // 2, t % 2
            part = res[:, t * 128 : (t + 1) * 128]
            for q in range(4):
                at = {"x": x, "y": y, "z": 2 * (q // 2) + zl}
                for k in range(3):
                    n = MAIN_N[k]
                    lo = q * 128 + MAIN_OFF[k] * 8
                    i0, i1, i2 = (at[a] for a in ORDERS[k])
                    main[k][q % 2, i0, i1, i2] = part[lo : lo + 8 * n].reshape(n, 8, 128)

    def chunk_send(i):
        y, x0 = i // 2, (i % 2) * 2
        out = []
        for k in range(3):
            r = region(k, y, x0)
            out.append(
                send(main[k].at[(1 - c,) + r], recv_core[k].at[r],
                     core_s.at[i * 3 + k], core_r.at[i * 3 + k], partner)
            )
        chunk_flights.append(out)

    def chunk_add(i):
        y, x0 = i // 2, (i % 2) * 2
        for k in range(3):
            chunk_flights[i][k].wait_recv()
            r = region(k, y, x0)
            main[k][(c,) + r] = main[k][(c,) + r] + recv_core[k][r]

    def top_tiles():
        def block(a, s):
            return keep[a * 128 : (a + 1) * 128, s * 128 : (s + 1) * 128]

        def put(i, v):
            top[i // 5, pl.ds((i % 5) * 16, 16)] = v.reshape(16, 8, 128)

        for base, (p, r) in ((0, (0, 1)), (7, (2, 3))):
            put(base, 0.5 * (block(p, p) + block(p, p).T))
            put(base + 1, 0.5 * (block(p, r) + block(r, p).T))
            put(base + 2, 0.5 * (block(r, r) + block(r, r).T))
        put(3, block(0, 2))
        put(4, block(1, 2))
        put(5, block(0, 3))
        put(6, block(1, 3))

    tbase = list(TOP_OFF)
    tflights = [[], [], []]

    def top_n(k, stage):
        return (TOP_N[k] * 4, TOP_N[k], TOP_N[k])[stage]

    def top_off(k, stage):
        return (TOP_OFF[k] // 4, TOP_OFF[k] // 16, TOP_OFF[k] // 16)[stage]

    def top_scatter(stage):
        dst = (t0, t1)[stage]
        for k in range(3):
            n, off, axis = top_n(k, stage), top_off(k, stage), ORDERS[k][stage]
            first = (stage * 3 + k) * 3
            tflights[k] = [
                send(tacc.at[pl.ds(tbase[k] + (pos[axis] + d) % 4 * n, n)],
                     dst.at[d - 1, pl.ds(off, n)],
                     tst_s.at[first + d - 1], tst_r.at[first + d - 1], peer(axis, d))
                for d in (1, 2, 3)
            ]

    def top_sum(stage):
        src = (t0, t1)[stage]
        for k in range(3):
            n, off, axis = top_n(k, stage), top_off(k, stage), ORDERS[k][stage]
            for cp in tflights[k]:
                cp.wait_recv()
            tbase[k] = tbase[k] + pos[axis] * n
            mine, sl = pl.ds(tbase[k], n), pl.ds(off, n)
            tacc[mine] = tacc[mine] + src[0, sl] + src[1, sl] + src[2, sl]

    def top_share():
        for k in range(3):
            n, off, axis = top_n(k, 2), top_off(k, 2), ORDERS[k][2]
            first = (6 + k) * 3
            tflights[k] = [
                send(tacc.at[pl.ds(tbase[k], n)], t2.at[d - 1, pl.ds(off, n)],
                     tst_s.at[first + d - 1], tst_r.at[first + d - 1], peer(axis, d))
                for d in (1, 2, 3)
            ]

    def top_total():
        for k in range(3):
            n, off = top_n(k, 2), top_off(k, 2)
            for cp in tflights[k]:
                cp.wait_recv()
            mine = pos[ORDERS[k][2]]
            parts = [tacc[pl.ds(tbase[k], n)]] + [t2[d, pl.ds(off, n)] for d in range(3)]
            vals = []
            for p in range(4):
                dist = (mine - p) % 4
                vals.append(jnp.where(
                    dist == 0, parts[0],
                    jnp.where(dist == 1, parts[1], jnp.where(dist == 2, parts[2], parts[3])),
                ))
            gat[c, pl.ds(tbase[k], n)] = (vals[0] + vals[1]) + (vals[2] + vals[3])

    def top_gather(stage):
        for k in range(3):
            n = TOP_N[k] * (1 if stage == 1 else 4)
            if stage == 0:
                tbase[k] = tbase[k] - pos[ORDERS[k][1]] * TOP_N[k]
            piece = gat.at[c, pl.ds(tbase[k], n)]
            first = ((1 - stage) * 3 + k) * 3
            tflights[k] = [
                send(piece, piece, ag_s.at[first + d - 1], ag_r.at[first + d - 1],
                     peer(ORDERS[k][stage], d))
                for d in (1, 2, 3)
            ]

    def top_wait():
        for k in range(3):
            for cp in tflights[k]:
                cp.wait_recv()

    def where(k, stage):
        return (c,) + tuple(pos[a] for a in ORDERS[k][:stage])

    def row_copy(stage, k, d):
        axis = ORDERS[k][stage]
        src = main[k].at[where(k, stage) + ((pos[axis] + d) % 4,)]
        dst = last_slots.at[d - 1, pl.ds(MAIN_OFF[k], MAIN_N[k])] if stage == 2 else slots[stage][k].at[d - 1]
        i = (stage * 3 + k) * 3 + d - 1
        return pltpu.make_async_remote_copy(
            src_ref=src, dst_ref=dst, send_sem=st_s.at[i], recv_sem=st_r.at[i],
            device_id=peer(axis, d), device_id_type=MESH,
        )

    def row_scatter(stage, k):
        for d in (1, 2, 3):
            row_copy(stage, k, d).start()

    def row_sum(stage, k):
        for d in (1, 2, 3):
            row_copy(stage, k, d).wait_recv()
        at = where(k, stage + 1)
        got = [
            last_slots[d, pl.ds(MAIN_OFF[k], MAIN_N[k])] if stage == 2 else slots[stage][k][d]
            for d in range(3)
        ]
        total_rows = (main[k][at] + got[0]) + (got[1] + got[2])
        if stage == 2:
            own[gi, pl.ds(MAIN_OFF[k], MAIN_N[k])] = total_rows
        else:
            main[k][at] = total_rows

    chunk(0)
    top_tiles()
    tcore = send(top.at[1 - c], ta, tcore_s, tcore_r, partner)
    chunk_send(0)
    chunk(1)
    chunk_send(1)
    tcore.wait_recv()
    tacc[...] = top[c] + ta[...]
    top_scatter(0)
    for i in (2, 3, 4):
        chunk(i)
        chunk_send(i)
    top_sum(0)
    top_scatter(1)
    for i in (5, 6, 7):
        chunk(i)
        chunk_send(i)
    top_sum(1)
    top_share()
    for i in range(8):
        chunk_add(i)
    top_total()
    top_gather(1)
    if EARLY_ROWS:
        for k in range(3):
            row_scatter(0, k)
    top_wait()
    top_gather(0)
    if not EARLY_ROWS:
        for k in range(3):
            row_scatter(0, k)
    top_wait()
    tlast = send(gat.at[c], gat.at[c], ag_s.at[18], ag_r.at[18], partner)
    tlast.wait_recv()

    row = lax.broadcasted_iota(jnp.int32, (128, 128), 0)
    lane = lax.broadcasted_iota(jnp.int32, (128, 128), 1)
    for i, (a, b) in enumerate(UPPER):
        v = gat[i // 5, pl.ds((i % 5) * 16, 16)].reshape(128, 128)
        if a == b:
            v = v + jnp.where(row == lane, hess_ref[a : a + 1, :], 0.0)
        aug[a * 128 : (a + 1) * 128, b * 128 : (b + 1) * 128] = v

    def step(j, _):
        @pl.when(j == 3)
        def _():
            for k in range(3):
                row_sum(0, k)
                row_scatter(1, k)

        at = pl.multiple_of(j * 128, 128)
        rows = pl.ds(at, 128)
        z = [aug[pl.ds(at + 8 * i, 8), pl.ds(at, 128)] for i in range(16)]
        z = inverse_factor(z)
        for i in range(16):
            linv[j, 8 * i : 8 * i + 8, :] = z[i]
        aug[rows, :] = dot(linv[j], aug[rows, :])

        def update(i, _):
            ai = pl.multiple_of(i * 128, 128)
            below = pl.ds(ai, 128)
            aug[below, :] = aug[below, :] - dot_t(aug[rows, pl.ds(ai, 128)], aug[rows, :])
            return 0

        lax.fori_loop(j + 1, 4, update, 0)
        return 0

    lax.fori_loop(0, 4, step, 0)
    for k in range(3):
        row_sum(1, k)
        row_scatter(2, k)
    for k in range(3):
        row_sum(2, k)
    mine = own.at[gi]
    flights = [
        send(mine, mine, ag_s.at[19 + j], ag_r.at[19 + j], dev)
        for j, dev in enumerate((partner, peer("z", 2), far))
    ]
    for cp in flights:
        cp.wait_recv()

    solved = []
    for j in range(4):
        acc = own[j].reshape(128, 128)
        for i in range(j):
            acc = acc - dot_t(aug[i * 128 : (i + 1) * 128, j * 128 : (j + 1) * 128], solved[i])
        solved.append(dot(linv[j], acc))
    at = pl.multiple_of(jnp.where(si < 4, si, 0) * 128, 128)
    for j in range(4):
        v = jnp.where(si < 4, aug[j * 128 : (j + 1) * 128, pl.ds(at, 128)], solved[j])
        v = jnp.where(j * 128 + row <= si * 128 + lane, v, 0.0)
        out_ref[:, j * 128 : (j + 1) * 128] = v.T
    for cp in pending:
        cp.wait_send()
    for stage in range(3):
        for k in range(3):
            for d in (1, 2, 3):
                row_copy(stage, k, d).wait_send()


EARLY_ROWS = True


def tail(hess, solved_t, coupling):
    tile = (8, 128)
    vm = lambda *lead: pltpu.VMEM(lead + tile, F32)
    sem = lambda n: pltpu.SemaphoreType.DMA((n,))
    vspec = pl.BlockSpec(memory_space=pltpu.VMEM)
    return pl.pallas_call(
        tail_kernel,
        in_specs=[vspec, vspec, pl.BlockSpec(memory_space=pl.ANY)],
        out_specs=vspec,
        out_shape=jax.ShapeDtypeStruct((128, 512), F32),
        scratch_shapes=[pltpu.VMEM((8, NB, 512), jnp.bfloat16)]
        + [vm(2, 4, 4, 4, n) for n in MAIN_N]
        + [vm(4, 4, 4, n) for n in MAIN_N]
        + [vm(3, 4, 4, n) for n in MAIN_N]
        + [vm(3, 4, n) for n in MAIN_N]
        + [
            vm(3, 16), vm(4, 16), pltpu.VMEM((512, 512), F32),
            vm(2, 80), vm(80), vm(80), vm(3, 20), vm(3, 5), vm(3, 5), vm(2, 80),
            pltpu.VMEM((512, 512), F32), pltpu.VMEM((4, 128, 128), F32),
            sem(8), sem(24), sem(24), pltpu.SemaphoreType.DMA, pltpu.SemaphoreType.DMA,
            sem(27), sem(27), sem(27), sem(27), sem(22), sem(22),
        ],
        compiler_params=pltpu.CompilerParams(
            collective_id=0, has_side_effects=True, vmem_limit_bytes=56 << 20
        ),
    )(hess, solved_t, coupling)


def per_device(coupling, scen_kkt, active_rows, first_hess):
    solved_t = scenario_solve(active_rows, scen_kkt[0], coupling[0])
    return tail(first_hess.reshape(4, 128), solved_t, coupling[0])


def solution(mesh):
    placed = (
        P(("scen", "grp"), None, None),
        P(("scen", "grp"), None, None),
        P(("scen", "grp")),
        P(),
    )
    return jax.shard_map(
        per_device, mesh=mesh, in_specs=placed, out_specs=P("scen", None), check_vma=False
    )
```

```python
import jax
import jax.numpy as jnp
from jax import lax
from jax.experimental import pallas as pl
from jax.experimental.pallas import tpu as pltpu
from jax.sharding import PartitionSpec as P

PW = 256
NC = 4096
NB = 768
F32 = jnp.float32
HIGHEST = lax.Precision.HIGHEST
MESH = pl.DeviceIdType.MESH

ORDERS = (("x", "y", "z"), ("y", "z", "x"), ("z", "x", "y"))
MAIN_N = (5, 5, 6)
MAIN_OFF = (0, 5, 10)
TOP_N = (2, 2, 1)
TOP_OFF = (0, 32, 64)


def total(terms):
    while len(terms) > 1:
        terms = [terms[i] + terms[i + 1] if i + 1 < len(terms) else terms[i] for i in range(0, len(terms), 2)]
    return terms[0]

def inverse_factor(z):
    shape = (8, 128)
    lane = lax.broadcasted_iota(jnp.int32, shape, 1)
    sub = lax.broadcasted_iota(jnp.int32, shape, 0)
    z = list(z)
    for j in range(16):
        lo = 8 * j
        zj = z[j]
        col = [jnp.broadcast_to(zj[:, lo + c : lo + c + 1], shape) for c in range(8)]
        e = {(r, c): jnp.broadcast_to(col[c][r : r + 1], shape) for c in range(8) for r in range(c, 8)}
        inv, l, t = {}, {}, {}
        for c in range(8):
            inv[c] = lax.rsqrt(e[c, c])
            for r in range(c + 1, 8):
                l[r, c] = e[r, c] * inv[c]
            for r in range(c + 1, 8):
                for q in range(c + 1, r + 1):
                    e[r, q] = e[r, q] - l[r, c] * l[q, c]
        for c in range(8):
            t[c, c] = inv[c]
            for r in range(c + 1, 8):
                t[r, c] = -inv[r] * total([l[r, m] * t[m, c] for m in range(c, r)])
        panel = (lane >= lo) & (lane < lo + 8)
        zp = jnp.where(panel, jnp.where(lane - lo == sub, 1.0, 0.0), zj)
        zb = [jnp.broadcast_to(zp[c : c + 1], shape) for c in range(8)]
        u = [total([t[r, c] * zb[c] for c in range(r + 1)]) for r in range(8)]
        w = [total([t[c, r] * u[c] for c in range(r, 8)]) for r in range(8)]
        row = u[0]
        for r in range(1, 8):
            row = jnp.where(sub == r, u[r], row)
        z[j] = jnp.where(lane < lo + 8, row, 0.0)
        for i in range(j + 1, 16):
            zi = z[i]
            q = [jnp.broadcast_to(zi[:, lo + c : lo + c + 1], shape) * w[c] for c in range(8)]
            z[i] = jnp.where(panel, 0.0, zi) - total(q)
    return z

def dot(a, b):
    return jnp.dot(a, b, precision=HIGHEST, preferred_element_type=F32)

def dot_t(a, b):
    return lax.dot_general(a, b, (((0,), (0,)), ((), ())), precision=HIGHEST, preferred_element_type=F32)

def solve_kernel(act_ref, k_ref, c_ref, st_ref, aug, linv, xs):
    row = lax.broadcasted_iota(jnp.int32, (NB, 1), 0)
    keep = (row < act_ref[0]).astype(F32)
    aug[:, :NB] = k_ref[...].astype(F32)
    aug[:, NB:] = c_ref[...].astype(F32) * keep

    def step(j, _):
        at = pl.multiple_of(j * 128, 128)
        rows = pl.ds(at, 128)
        z = [aug[pl.ds(at + 8 * i, 8), pl.ds(at, 128)] for i in range(16)]
        z = inverse_factor(z)
        for i in range(16):
            linv[j, 8 * i : 8 * i + 8, :] = z[i]
        y = dot(linv[j], aug[rows, :])
        aug[rows, :] = y

        def update(i, _):
            ai = pl.multiple_of(i * 128, 128)
            g = aug[rows, pl.ds(ai, 128)]
            below = pl.ds(ai, 128)
            aug[below, :] = aug[below, :] - dot_t(g, aug[rows, :])
            return 0

        lax.fori_loop(j + 1, NB // 128, update, 0)
        return 0

    lax.fori_loop(0, NB // 128, step, 0)
    for j in range(NB // 128 - 1, -1, -1):
        lo, hi = j * 128, j * 128 + 128
        acc = aug[lo:hi, NB:]
        if hi < NB:
            acc = acc - dot(aug[lo:hi, hi:NB], xs[hi:, :])
        x = dot_t(linv[j], acc)
        xs[lo:hi, :] = x
        st_ref[:, lo:hi] = (x * keep[lo:hi]).T.astype(jnp.bfloat16)

def scenario_solve(active, kkt, coupling):
    vspec = pl.BlockSpec(memory_space=pltpu.VMEM)
    return pl.pallas_call(
        solve_kernel,
        grid=(1,),
        in_specs=[pl.BlockSpec(memory_space=pltpu.SMEM), pl.BlockSpec((NB, NB), lambda i: (0, 0)),
                  pl.BlockSpec((NB, 512), lambda i: (0, 0))],
        out_specs=pl.BlockSpec((512, NB), lambda i: (0, 0)),
        out_shape=jax.ShapeDtypeStruct((512, NB), jnp.bfloat16),
        scratch_shapes=[pltpu.VMEM((NB, 1280), F32), pltpu.VMEM((6, 128, 128), F32), pltpu.VMEM((NB, 512), F32)],
        compiler_params=pltpu.CompilerParams(vmem_limit_bytes=48 << 20),
    )(active, kkt, coupling)


UPPER = ((0, 0), (0, 1), (1, 1), (0, 2), (1, 2), (0, 3), (1, 3), (2, 2), (2, 3), (3, 3))


def tail_kernel(
    hess_ref, st_ref, coup_ref, out_ref,
    cbuf, ma, mb, mc, ra, rb, rc, pa, pb, pc, qa, qb, qc, last_slots, own,
    keep, top, tacc, ta, t0, t1, t2, gat, aug, linv,
    c_sem, core_s, core_r, tcore_s, tcore_r, st_s, st_r, tst_s, tst_r, ag_s, ag_r,
):
    si = lax.axis_index("scen")
    gi = lax.axis_index("grp")
    c = gi % 2
    zh = gi // 2
    pos = {"y": si // 8, "x": (si // 2) % 4, "z": 2 * zh + si % 2}
    main, recv_core = (ma, mb, mc), (ra, rb, rc)
    slots = ((pa, pb, pc), (qa, qb, qc))

    loads = [
        pltpu.make_async_copy(coup_ref.at[:, pl.ds(i * 512, 512)], cbuf.at[i], c_sem.at[i])
        for i in range(8)
    ]
    for cp in loads:
        cp.start()

    def device(y, x, z, core):
        return {"scen": (y * 4 + x) * 2 + z % 2, "grp": (z // 2) * 2 + core}

    def peer(axis, dist):
        at = dict(pos)
        at[axis] = (at[axis] + dist) % 4
        return device(at["y"], at["x"], at["z"], c)

    partner = device(pos["y"], pos["x"], pos["z"], 1 - c)
    far = device(pos["y"], pos["x"], (pos["z"] + 2) % 4, 1 - c)

    barrier = pltpu.get_barrier_semaphore()
    greet = [peer(a, d) for a in "xyz" for d in (1, 2, 3)] + [partner, far]
    for dev in greet:
        pl.semaphore_signal(barrier, inc=1, device_id=dev, device_id_type=MESH)
    pl.semaphore_wait(barrier, len(greet))

    pending = []

    def send(src, dst, ssem, rsem, dev):
        cp = pltpu.make_async_remote_copy(
            src_ref=src, dst_ref=dst, send_sem=ssem, recv_sem=rsem,
            device_id=dev, device_id_type=MESH,
        )
        cp.start()
        pending.append(cp)
        return cp

    chunk_flights = []

    def region(k, y, x0):
        at = {"x": pl.ds(x0, 2), "y": y, "z": pl.ds(0, 4)}
        return tuple(at[a] for a in ORDERS[k])

    def chunk(i):
        y, x0 = i // 2, (i % 2) * 2
        loads[i].wait()
        res = jnp.dot(st_ref[...], cbuf[i], preferred_element_type=F32)
        if i == 0:
            keep[...] = res
        for t in range(4):
            x, zl = x0 + t // 2, t % 2
            part = res[:, t * 128 : (t + 1) * 128]
            for q in range(4):
                at = {"x": x, "y": y, "z": 2 * (q // 2) + zl}
                for k in range(3):
                    n = MAIN_N[k]
                    lo = q * 128 + MAIN_OFF[k] * 8
                    i0, i1, i2 = (at[a] for a in ORDERS[k])
                    main[k][q % 2, i0, i1, i2] = part[lo : lo + 8 * n].reshape(n, 8, 128)

    def chunk_send(i):
        y, x0 = i // 2, (i % 2) * 2
        out = []
        for k in range(3):
            r = region(k, y, x0)
            out.append(
                send(main[k].at[(1 - c,) + r], recv_core[k].at[r],
                     core_s.at[i * 3 + k], core_r.at[i * 3 + k], partner)
            )
        chunk_flights.append(out)

    def chunk_add(i):
        y, x0 = i // 2, (i % 2) * 2
        for k in range(3):
            chunk_flights[i][k].wait_recv()
            r = region(k, y, x0)
            main[k][(c,) + r] = main[k][(c,) + r] + recv_core[k][r]

    def top_tiles():
        def block(a, s):
            return keep[a * 128 : (a + 1) * 128, s * 128 : (s + 1) * 128]

        def put(i, v):
            top[i // 5, pl.ds((i % 5) * 16, 16)] = v.reshape(16, 8, 128)

        for base, (p, r) in ((0, (0, 1)), (7, (2, 3))):
            put(base, 0.5 * (block(p, p) + block(p, p).T))
            put(base + 1, 0.5 * (block(p, r) + block(r, p).T))
            put(base + 2, 0.5 * (block(r, r) + block(r, r).T))
        put(3, block(0, 2))
        put(4, block(1, 2))
        put(5, block(0, 3))
        put(6, block(1, 3))

    tbase = list(TOP_OFF)
    tflights = [[], [], []]

    def top_n(k, stage):
        return (TOP_N[k] * 4, TOP_N[k], TOP_N[k])[stage]

    def top_off(k, stage):
        return (TOP_OFF[k] // 4, TOP_OFF[k] // 16, TOP_OFF[k] // 16)[stage]

    def top_scatter(stage):
        dst = (t0, t1)[stage]
        for k in range(3):
            n, off, axis = top_n(k, stage), top_off(k, stage), ORDERS[k][stage]
            first = (stage * 3 + k) * 3
            tflights[k] = [
                send(tacc.at[pl.ds(tbase[k] + (pos[axis] + d) % 4 * n, n)],
                     dst.at[d - 1, pl.ds(off, n)],
                     tst_s.at[first + d - 1], tst_r.at[first + d - 1], peer(axis, d))
                for d in (1, 2, 3)
            ]

    def top_sum(stage):
        src = (t0, t1)[stage]
        for k in range(3):
            n, off, axis = top_n(k, stage), top_off(k, stage), ORDERS[k][stage]
            for cp in tflights[k]:
                cp.wait_recv()
            tbase[k] = tbase[k] + pos[axis] * n
            mine, sl = pl.ds(tbase[k], n), pl.ds(off, n)
            tacc[mine] = tacc[mine] + src[0, sl] + src[1, sl] + src[2, sl]

    def top_share():
        for k in range(3):
            n, off, axis = top_n(k, 2), top_off(k, 2), ORDERS[k][2]
            first = (6 + k) * 3
            tflights[k] = [
                send(tacc.at[pl.ds(tbase[k], n)], t2.at[d - 1, pl.ds(off, n)],
                     tst_s.at[first + d - 1], tst_r.at[first + d - 1], peer(axis, d))
                for d in (1, 2, 3)
            ]

    def top_total():
        for k in range(3):
            n, off = top_n(k, 2), top_off(k, 2)
            for cp in tflights[k]:
                cp.wait_recv()
            mine = pos[ORDERS[k][2]]
            parts = [tacc[pl.ds(tbase[k], n)]] + [t2[d, pl.ds(off, n)] for d in range(3)]
            vals = []
            for p in range(4):
                dist = (mine - p) % 4
                vals.append(jnp.where(
                    dist == 0, parts[0],
                    jnp.where(dist == 1, parts[1], jnp.where(dist == 2, parts[2], parts[3])),
                ))
            gat[c, pl.ds(tbase[k], n)] = (vals[0] + vals[1]) + (vals[2] + vals[3])

    def top_gather(stage):
        for k in range(3):
            n = TOP_N[k] * (1 if stage == 1 else 4)
            if stage == 0:
                tbase[k] = tbase[k] - pos[ORDERS[k][1]] * TOP_N[k]
            piece = gat.at[c, pl.ds(tbase[k], n)]
            first = ((1 - stage) * 3 + k) * 3
            tflights[k] = [
                send(piece, piece, ag_s.at[first + d - 1], ag_r.at[first + d - 1],
                     peer(ORDERS[k][stage], d))
                for d in (1, 2, 3)
            ]

    def top_wait():
        for k in range(3):
            for cp in tflights[k]:
                cp.wait_recv()

    def where(k, stage):
        return (c,) + tuple(pos[a] for a in ORDERS[k][:stage])

    def row_copy(stage, k, d):
        axis = ORDERS[k][stage]
        src = main[k].at[where(k, stage) + ((pos[axis] + d) % 4,)]
        dst = last_slots.at[d - 1, pl.ds(MAIN_OFF[k], MAIN_N[k])] if stage == 2 else slots[stage][k].at[d - 1]
        i = (stage * 3 + k) * 3 + d - 1
        return pltpu.make_async_remote_copy(
            src_ref=src, dst_ref=dst, send_sem=st_s.at[i], recv_sem=st_r.at[i],
            device_id=peer(axis, d), device_id_type=MESH,
        )

    def row_scatter(stage, k):
        for d in (1, 2, 3):
            row_copy(stage, k, d).start()

    def row_sum(stage, k):
        for d in (1, 2, 3):
            row_copy(stage, k, d).wait_recv()
        at = where(k, stage + 1)
        got = [
            last_slots[d, pl.ds(MAIN_OFF[k], MAIN_N[k])] if stage == 2 else slots[stage][k][d]
            for d in range(3)
        ]
        total_rows = (main[k][at] + got[0]) + (got[1] + got[2])
        if stage == 2:
            own[gi, pl.ds(MAIN_OFF[k], MAIN_N[k])] = total_rows
        else:
            main[k][at] = total_rows

    chunk(0)
    top_tiles()
    tcore = send(top.at[1 - c], ta, tcore_s, tcore_r, partner)
    chunk_send(0)
    chunk(1)
    chunk_send(1)
    tcore.wait_recv()
    tacc[...] = top[c] + ta[...]
    top_scatter(0)
    for i in (2, 3, 4):
        chunk(i)
        chunk_send(i)
    top_sum(0)
    top_scatter(1)
    for i in (5, 6, 7):
        chunk(i)
        chunk_send(i)
    top_sum(1)
    top_share()
    for i in range(8):
        chunk_add(i)
    top_total()
    top_gather(1)
    top_wait()
    top_gather(0)
    for k in range(3):
        row_scatter(0, k)
    top_wait()
    tlast = send(gat.at[c], gat.at[c], ag_s.at[18], ag_r.at[18], partner)
    tlast.wait_recv()

    row = lax.broadcasted_iota(jnp.int32, (128, 128), 0)
    lane = lax.broadcasted_iota(jnp.int32, (128, 128), 1)
    for i, (a, b) in enumerate(UPPER):
        v = gat[i // 5, pl.ds((i % 5) * 16, 16)].reshape(128, 128)
        if a == b:
            v = v + jnp.where(row == lane, hess_ref[a : a + 1, :], 0.0)
        aug[a * 128 : (a + 1) * 128, b * 128 : (b + 1) * 128] = v

    def step(j, _):
        @pl.when(j == 2)
        def _():
            for k in range(3):
                row_sum(0, k)
                row_scatter(1, k)

        @pl.when(j == 3)
        def _():
            for k in range(3):
                row_sum(1, k)
                row_scatter(2, k)

        at = pl.multiple_of(j * 128, 128)
        rows = pl.ds(at, 128)
        z = [aug[pl.ds(at + 8 * i, 8), pl.ds(at, 128)] for i in range(16)]
        z = inverse_factor(z)
        for i in range(16):
            linv[j, 8 * i : 8 * i + 8, :] = z[i]
        aug[rows, :] = dot(linv[j], aug[rows, :])

        def update(i, _):
            ai = pl.multiple_of(i * 128, 128)
            below = pl.ds(ai, 128)
            aug[below, :] = aug[below, :] - dot_t(aug[rows, pl.ds(ai, 128)], aug[rows, :])
            return 0

        lax.fori_loop(j + 1, 4, update, 0)
        return 0

    lax.fori_loop(0, 4, step, 0)
    for k in range(3):
        row_sum(2, k)
    mine = own.at[gi]
    flights = [
        send(mine, mine, ag_s.at[19 + j], ag_r.at[19 + j], dev)
        for j, dev in enumerate((partner, peer("z", 2), far))
    ]
    for cp in flights:
        cp.wait_recv()

    solved = []
    for j in range(4):
        acc = own[j].reshape(128, 128)
        for i in range(j):
            acc = acc - dot_t(aug[i * 128 : (i + 1) * 128, j * 128 : (j + 1) * 128], solved[i])
        solved.append(dot(linv[j], acc))
    at = pl.multiple_of(jnp.where(si < 4, si, 0) * 128, 128)
    for j in range(4):
        v = jnp.where(si < 4, aug[j * 128 : (j + 1) * 128, pl.ds(at, 128)], solved[j])
        v = jnp.where(j * 128 + row <= si * 128 + lane, v, 0.0)
        out_ref[:, j * 128 : (j + 1) * 128] = v.T
    for cp in pending:
        cp.wait_send()
    for stage in range(3):
        for k in range(3):
            for d in (1, 2, 3):
                row_copy(stage, k, d).wait_send()


def tail(hess, solved_t, coupling):
    tile = (8, 128)
    vm = lambda *lead: pltpu.VMEM(lead + tile, F32)
    sem = lambda n: pltpu.SemaphoreType.DMA((n,))
    vspec = pl.BlockSpec(memory_space=pltpu.VMEM)
    return pl.pallas_call(
        tail_kernel,
        in_specs=[vspec, vspec, pl.BlockSpec(memory_space=pl.ANY)],
        out_specs=vspec,
        out_shape=jax.ShapeDtypeStruct((128, 512), F32),
        scratch_shapes=[pltpu.VMEM((8, NB, 512), jnp.bfloat16)]
        + [vm(2, 4, 4, 4, n) for n in MAIN_N]
        + [vm(4, 4, 4, n) for n in MAIN_N]
        + [vm(3, 4, 4, n) for n in MAIN_N]
        + [vm(3, 4, n) for n in MAIN_N]
        + [
            vm(3, 16), vm(4, 16), pltpu.VMEM((512, 512), F32),
            vm(2, 80), vm(80), vm(80), vm(3, 20), vm(3, 5), vm(3, 5), vm(2, 80),
            pltpu.VMEM((512, 512), F32), pltpu.VMEM((4, 128, 128), F32),
            sem(8), sem(24), sem(24), pltpu.SemaphoreType.DMA, pltpu.SemaphoreType.DMA,
            sem(27), sem(27), sem(27), sem(27), sem(22), sem(22),
        ],
        compiler_params=pltpu.CompilerParams(
            collective_id=0, has_side_effects=True, vmem_limit_bytes=56 << 20
        ),
    )(hess, solved_t, coupling)


def per_device(coupling, scen_kkt, active_rows, first_hess):
    solved_t = scenario_solve(active_rows, scen_kkt[0], coupling[0])
    return tail(first_hess.reshape(4, 128), solved_t, coupling[0])


def solution(mesh):
    placed = (
        P(("scen", "grp"), None, None),
        P(("scen", "grp"), None, None),
        P(("scen", "grp")),
        P(),
    )
    return jax.shard_map(
        per_device, mesh=mesh, in_specs=placed, out_specs=P("scen", None), check_vma=False
    )
```

```python
import jax
import jax.numpy as jnp
from jax import lax
from jax.experimental import pallas as pl
from jax.experimental.pallas import tpu as pltpu
from jax.sharding import PartitionSpec as P

PW = 256
NC = 4096
NB = 768
F32 = jnp.float32
MESH = pl.DeviceIdType.MESH

ORDERS = (("x", "y", "z"), ("y", "z", "x"), ("z", "x", "y"))
MAIN_N = (5, 5, 6)
MAIN_OFF = (0, 5, 10)
TOP_N = (2, 2, 1)
TOP_OFF = (0, 32, 64)


def total(terms):
    while len(terms) > 1:
        terms = [terms[i] + terms[i + 1] if i + 1 < len(terms) else terms[i] for i in range(0, len(terms), 2)]
    return terms[0]

def pair_factor(e):
    inv, l, t = {}, {}, {}
    for c in range(0, 8, 2):
        d = c + 1
        a = e[c, c]
        b = e[d, c]
        ra = lax.rsqrt(a)
        rd = lax.rsqrt(a * e[d, d] - b * b)
        inv[c] = ra
        inv[d] = (a * ra) * rd
        l[d, c] = b * ra
        for r in range(c + 2, 8):
            l[r, c] = e[r, c] * ra
            l[r, d] = (e[r, d] - l[r, c] * l[d, c]) * inv[d]
        for r in range(c + 2, 8):
            for q in range(c + 2, r + 1):
                e[r, q] = (e[r, q] - l[r, c] * l[q, c]) - l[r, d] * l[q, d]
    return inv, l


def bc(x, r):
    return jnp.broadcast_to(x[r : r + 1, :], (8, 128))


def inverse_factor(z):
    shape = (8, 128)
    lane = lax.broadcasted_iota(jnp.int32, shape, 1)
    sub = lax.broadcasted_iota(jnp.int32, shape, 0)
    z = list(z)
    for j in range(16):
        lo = 8 * j
        zj = z[j]
        panel = (lane >= lo) & (lane < lo + 8)
        zp = jnp.where(panel, jnp.where(lane - lo == sub, 1.0, 0.0), zj)
        rows = [bc(zj, r) for r in range(8)]
        zero = jnp.zeros(shape, F32)
        e = {(r, c): jnp.broadcast_to((rows[r] + zero)[:, lo + c : lo + c + 1], shape) for c in range(8) for r in range(c, 8)}
        inv, l = pair_factor(e)
        t = {}
        for c in range(8):
            t[c, c] = inv[c]
            for r in range(c + 1, 8):
                t[r, c] = -inv[r] * total([l[r, m] * t[m, c] for m in range(c, r)])
        zb = [bc(zp, c) for c in range(8)]
        u = [total([t[r, c] * zb[c] for c in range(r + 1)]) for r in range(8)]
        w = [total([t[c, r] * u[c] for c in range(r, 8)]) for r in range(8)]
        row = u[0]
        for r in range(1, 8):
            row = jnp.where(sub == r, u[r], row)
        z[j] = jnp.where(lane < lo + 8, row, 0.0)
        for i in range(j + 1, 16):
            zi = z[i]
            q = [jnp.broadcast_to(zi[:, lo + c : lo + c + 1], shape) * w[c] for c in range(8)]
            z[i] = jnp.where(panel, 0.0, zi) - total(q)
    return z


BF16 = jnp.bfloat16

def halves(a):
    hi = a.astype(BF16)
    return hi, (a - hi.astype(F32)).astype(BF16)

def left(a, axis):
    hi, lo = halves(a)
    return jnp.concatenate([hi, lo, hi], axis)

def right(a):
    hi, lo = halves(a)
    return jnp.concatenate([hi, hi, lo], 0)

def dot(a, b):
    return jnp.dot(left(a, 1), right(b), preferred_element_type=F32)

def dot_t(a, b):
    return lax.dot_general(left(a, 0), right(b), (((0,), (0,)), ((), ())), preferred_element_type=F32)

def solve_kernel(act_ref, k_ref, c_ref, st_ref, aug, linv, xs, yl, yr):
    row = lax.broadcasted_iota(jnp.int32, (NB, 1), 0)
    keep = (row < act_ref[0]).astype(F32)
    aug[:, :NB] = k_ref[...].astype(F32)
    aug[:, NB:] = c_ref[...].astype(F32) * keep

    def step(j, _):
        at = pl.multiple_of(j * 128, 128)
        rows = pl.ds(at, 128)
        z = [aug[pl.ds(at + 8 * i, 8), pl.ds(at, 128)] for i in range(16)]
        z = inverse_factor(z)
        for i in range(16):
            linv[j, 8 * i : 8 * i + 8, :] = z[i]
        y = dot(linv[j], aug[rows, :])
        aug[rows, :] = y
        hi, lo = halves(y)
        yl[0:128] = hi[:, :NB]
        yl[128:256] = lo[:, :NB]
        yl[256:384] = hi[:, :NB]
        yr[0:128] = hi
        yr[128:256] = hi
        yr[256:384] = lo

        def update(i, _):
            ai = pl.multiple_of(i * 128, 128)
            below = pl.ds(ai, 128)
            aug[below, :] = aug[below, :] - lax.dot_general(
                yl[:, pl.ds(ai, 128)], yr[...], (((0,), (0,)), ((), ())), preferred_element_type=F32
            )
            return 0

        lax.fori_loop(j + 1, NB // 128, update, 0)
        return 0

    lax.fori_loop(0, NB // 128, step, 0)
    for j in range(NB // 128 - 1, -1, -1):
        lo, hi = j * 128, j * 128 + 128
        acc = aug[lo:hi, NB:]
        if hi < NB:
            acc = acc - dot(aug[lo:hi, hi:NB], xs[hi:, :])
        x = dot_t(linv[j], acc)
        xs[lo:hi, :] = x
        st_ref[:, lo:hi] = (x * keep[lo:hi]).T.astype(jnp.bfloat16)

def scenario_solve(active, kkt, coupling):
    vspec = pl.BlockSpec(memory_space=pltpu.VMEM)
    return pl.pallas_call(
        solve_kernel,
        grid=(1,),
        in_specs=[pl.BlockSpec(memory_space=pltpu.SMEM), pl.BlockSpec((NB, NB), lambda i: (0, 0)),
                  pl.BlockSpec((NB, 512), lambda i: (0, 0))],
        out_specs=pl.BlockSpec((512, NB), lambda i: (0, 0)),
        out_shape=jax.ShapeDtypeStruct((512, NB), jnp.bfloat16),
        scratch_shapes=[pltpu.VMEM((NB, 1280), F32), pltpu.VMEM((6, 128, 128), F32), pltpu.VMEM((NB, 512), F32),
                        pltpu.VMEM((384, NB), BF16), pltpu.VMEM((384, 1280), BF16)],
        compiler_params=pltpu.CompilerParams(vmem_limit_bytes=48 << 20),
    )(active, kkt, coupling)


UPPER = ((0, 0), (0, 1), (1, 1), (0, 2), (1, 2), (0, 3), (1, 3), (2, 2), (2, 3), (3, 3))


def tail_kernel(
    hess_ref, st_ref, coup_ref, out_ref,
    cbuf, ma, mb, mc, ra, rb, rc, pa, pb, pc, qa, qb, qc, last_slots, own,
    keep, top, tacc, ta, t0, t1, t2, gat, aug, linv, sol,
    c_sem, core_s, core_r, tcore_s, tcore_r, st_s, st_r, tst_s, tst_r, ag_s, ag_r,
):
    si = lax.axis_index("scen")
    gi = lax.axis_index("grp")
    c = gi % 2
    zh = gi // 2
    pos = {"y": si // 8, "x": (si // 2) % 4, "z": 2 * zh + si % 2}
    main, recv_core = (ma, mb, mc), (ra, rb, rc)
    slots = ((pa, pb, pc), (qa, qb, qc))

    loads = [
        pltpu.make_async_copy(coup_ref.at[:, pl.ds(i * 512, 512)], cbuf.at[i], c_sem.at[i])
        for i in range(8)
    ]
    for cp in loads:
        cp.start()

    def device(y, x, z, core):
        return {"scen": (y * 4 + x) * 2 + z % 2, "grp": (z // 2) * 2 + core}

    def peer(axis, dist):
        at = dict(pos)
        at[axis] = (at[axis] + dist) % 4
        return device(at["y"], at["x"], at["z"], c)

    partner = device(pos["y"], pos["x"], pos["z"], 1 - c)
    far = device(pos["y"], pos["x"], (pos["z"] + 2) % 4, 1 - c)

    barrier = pltpu.get_barrier_semaphore()
    greet = [peer(a, d) for a in "xyz" for d in (1, 2, 3)] + [partner, far]
    for dev in greet:
        pl.semaphore_signal(barrier, inc=1, device_id=dev, device_id_type=MESH)
    pl.semaphore_wait(barrier, len(greet))

    pending = []

    def send(src, dst, ssem, rsem, dev):
        cp = pltpu.make_async_remote_copy(
            src_ref=src, dst_ref=dst, send_sem=ssem, recv_sem=rsem,
            device_id=dev, device_id_type=MESH,
        )
        cp.start()
        pending.append(cp)
        return cp

    chunk_flights = []

    def region(k, y, x0):
        at = {"x": pl.ds(x0, 2), "y": y, "z": pl.ds(0, 4)}
        return tuple(at[a] for a in ORDERS[k])

    def chunk(i):
        y, x0 = i // 2, (i % 2) * 2
        loads[i].wait()
        res = jnp.dot(st_ref[...], cbuf[i], preferred_element_type=F32)
        if i == 0:
            keep[...] = res
        for t in range(4):
            x, zl = x0 + t // 2, t % 2
            part = res[:, t * 128 : (t + 1) * 128]
            for q in range(4):
                at = {"x": x, "y": y, "z": 2 * (q // 2) + zl}
                for k in range(3):
                    n = MAIN_N[k]
                    lo = q * 128 + MAIN_OFF[k] * 8
                    i0, i1, i2 = (at[a] for a in ORDERS[k])
                    main[k][q % 2, i0, i1, i2] = part[lo : lo + 8 * n].reshape(n, 8, 128)

    def chunk_send(i):
        y, x0 = i // 2, (i % 2) * 2
        out = []
        for k in range(3):
            r = region(k, y, x0)
            out.append(
                send(main[k].at[(1 - c,) + r], recv_core[k].at[r],
                     core_s.at[i * 3 + k], core_r.at[i * 3 + k], partner)
            )
        chunk_flights.append(out)

    def chunk_add(i):
        y, x0 = i // 2, (i % 2) * 2
        for k in range(3):
            chunk_flights[i][k].wait_recv()
            r = region(k, y, x0)
            main[k][(c,) + r] = main[k][(c,) + r] + recv_core[k][r]

    def top_tiles():
        def block(a, s):
            return keep[a * 128 : (a + 1) * 128, s * 128 : (s + 1) * 128]

        def put(i, v):
            top[i // 5, pl.ds((i % 5) * 16, 16)] = v.reshape(16, 8, 128)

        for base, (p, r) in ((0, (0, 1)), (7, (2, 3))):
            put(base, 0.5 * (block(p, p) + block(p, p).T))
            put(base + 1, 0.5 * (block(p, r) + block(r, p).T))
            put(base + 2, 0.5 * (block(r, r) + block(r, r).T))
        put(3, block(0, 2))
        put(4, block(1, 2))
        put(5, block(0, 3))
        put(6, block(1, 3))

    tbase = list(TOP_OFF)
    tflights = [[], [], []]

    def top_n(k, stage):
        return (TOP_N[k] * 4, TOP_N[k], TOP_N[k])[stage]

    def top_off(k, stage):
        return (TOP_OFF[k] // 4, TOP_OFF[k] // 16, TOP_OFF[k] // 16)[stage]

    def top_scatter(stage):
        dst = (t0, t1)[stage]
        for k in range(3):
            n, off, axis = top_n(k, stage), top_off(k, stage), ORDERS[k][stage]
            first = (stage * 3 + k) * 3
            tflights[k] = [
                send(tacc.at[pl.ds(tbase[k] + (pos[axis] + d) % 4 * n, n)],
                     dst.at[d - 1, pl.ds(off, n)],
                     tst_s.at[first + d - 1], tst_r.at[first + d - 1], peer(axis, d))
                for d in (1, 2, 3)
            ]

    def top_sum(stage):
        src = (t0, t1)[stage]
        for k in range(3):
            n, off, axis = top_n(k, stage), top_off(k, stage), ORDERS[k][stage]
            for cp in tflights[k]:
                cp.wait_recv()
            tbase[k] = tbase[k] + pos[axis] * n
            mine, sl = pl.ds(tbase[k], n), pl.ds(off, n)
            tacc[mine] = tacc[mine] + src[0, sl] + src[1, sl] + src[2, sl]

    def top_share():
        for k in range(3):
            n, off, axis = top_n(k, 2), top_off(k, 2), ORDERS[k][2]
            first = (6 + k) * 3
            tflights[k] = [
                send(tacc.at[pl.ds(tbase[k], n)], t2.at[d - 1, pl.ds(off, n)],
                     tst_s.at[first + d - 1], tst_r.at[first + d - 1], peer(axis, d))
                for d in (1, 2, 3)
            ]

    def top_total():
        for k in range(3):
            n, off = top_n(k, 2), top_off(k, 2)
            for cp in tflights[k]:
                cp.wait_recv()
            mine = pos[ORDERS[k][2]]
            parts = [tacc[pl.ds(tbase[k], n)]] + [t2[d, pl.ds(off, n)] for d in range(3)]
            vals = []
            for p in range(4):
                dist = (mine - p) % 4
                vals.append(jnp.where(
                    dist == 0, parts[0],
                    jnp.where(dist == 1, parts[1], jnp.where(dist == 2, parts[2], parts[3])),
                ))
            gat[c, pl.ds(tbase[k], n)] = (vals[0] + vals[1]) + (vals[2] + vals[3])

    def top_gather(stage):
        for k in range(3):
            n = TOP_N[k] * (1 if stage == 1 else 4)
            if stage == 0:
                tbase[k] = tbase[k] - pos[ORDERS[k][1]] * TOP_N[k]
            piece = gat.at[c, pl.ds(tbase[k], n)]
            first = ((1 - stage) * 3 + k) * 3
            tflights[k] = [
                send(piece, piece, ag_s.at[first + d - 1], ag_r.at[first + d - 1],
                     peer(ORDERS[k][stage], d))
                for d in (1, 2, 3)
            ]

    def top_wait():
        for k in range(3):
            for cp in tflights[k]:
                cp.wait_recv()

    def where(k, stage):
        return (c,) + tuple(pos[a] for a in ORDERS[k][:stage])

    def row_copy(stage, k, d):
        axis = ORDERS[k][stage]
        src = main[k].at[where(k, stage) + ((pos[axis] + d) % 4,)]
        dst = last_slots.at[d - 1, pl.ds(MAIN_OFF[k], MAIN_N[k])] if stage == 2 else slots[stage][k].at[d - 1]
        i = (stage * 3 + k) * 3 + d - 1
        return pltpu.make_async_remote_copy(
            src_ref=src, dst_ref=dst, send_sem=st_s.at[i], recv_sem=st_r.at[i],
            device_id=peer(axis, d), device_id_type=MESH,
        )

    def row_scatter(stage, k):
        for d in (1, 2, 3):
            row_copy(stage, k, d).start()

    def row_sum(stage, k):
        for d in (1, 2, 3):
            row_copy(stage, k, d).wait_recv()
        at = where(k, stage + 1)
        got = [
            last_slots[d, pl.ds(MAIN_OFF[k], MAIN_N[k])] if stage == 2 else slots[stage][k][d]
            for d in range(3)
        ]
        total_rows = (main[k][at] + got[0]) + (got[1] + got[2])
        if stage == 2:
            own[gi, pl.ds(MAIN_OFF[k], MAIN_N[k])] = total_rows
        else:
            main[k][at] = total_rows

    chunk(0)
    top_tiles()
    tcore = send(top.at[1 - c], ta, tcore_s, tcore_r, partner)
    chunk_send(0)
    chunk(1)
    chunk_send(1)
    tcore.wait_recv()
    tacc[...] = top[c] + ta[...]
    top_scatter(0)
    for i in (2, 3, 4):
        chunk(i)
        chunk_send(i)
    top_sum(0)
    top_scatter(1)
    for i in (5, 6, 7):
        chunk(i)
        chunk_send(i)
    top_sum(1)
    top_share()
    for i in range(8):
        chunk_add(i)
    top_total()
    top_gather(1)
    top_wait()
    top_gather(0)
    for k in range(3):
        row_scatter(0, k)
    top_wait()
    tlast = send(gat.at[c], gat.at[c], ag_s.at[18], ag_r.at[18], partner)
    tlast.wait_recv()

    row = lax.broadcasted_iota(jnp.int32, (128, 128), 0)
    lane = lax.broadcasted_iota(jnp.int32, (128, 128), 1)
    for i, (a, b) in enumerate(UPPER):
        v = gat[i // 5, pl.ds((i % 5) * 16, 16)].reshape(128, 128)
        if a == b:
            v = v + jnp.where(row == lane, hess_ref[a : a + 1, :], 0.0)
        aug[a * 128 : (a + 1) * 128, b * 128 : (b + 1) * 128] = v

    def step(j, _):
        @pl.when(j == 2)
        def _():
            for k in range(3):
                row_sum(0, k)
                row_scatter(1, k)

        @pl.when(j == 3)
        def _():
            for k in range(3):
                row_sum(1, k)
                row_scatter(2, k)

        at = pl.multiple_of(j * 128, 128)
        rows = pl.ds(at, 128)
        z = [aug[pl.ds(at + 8 * i, 8), pl.ds(at, 128)] for i in range(16)]
        z = inverse_factor(z)
        for i in range(16):
            linv[j, 8 * i : 8 * i + 8, :] = z[i]
        aug[rows, :] = dot(linv[j], aug[rows, :])

        def update(i, _):
            ai = pl.multiple_of(i * 128, 128)
            below = pl.ds(ai, 128)
            aug[below, :] = aug[below, :] - dot_t(aug[rows, pl.ds(ai, 128)], aug[rows, :])
            return 0

        lax.fori_loop(j + 1, 4, update, 0)
        return 0

    lax.fori_loop(0, 4, step, 0)
    for k in range(3):
        row_sum(2, k)
    mine = own.at[gi]
    flights = [
        send(mine, mine, ag_s.at[19 + j], ag_r.at[19 + j], dev)
        for j, dev in enumerate((partner, peer("z", 2), far))
    ]
    for cp in flights:
        cp.wait_recv()

    for j in range(4):
        lo, hi = j * 128, j * 128 + 128
        acc = own[j].reshape(128, 128)
        if j:
            acc = acc - dot_t(aug[:lo, lo:hi], sol[:lo, :])
        sol[lo:hi, :] = dot(linv[j], acc)
    at = pl.multiple_of(jnp.where(si < 4, si, 0) * 128, 128)
    for j in range(4):
        v = jnp.where(si < 4, aug[j * 128 : (j + 1) * 128, pl.ds(at, 128)], sol[j * 128 : (j + 1) * 128, :])
        v = jnp.where(j * 128 + row <= si * 128 + lane, v, 0.0)
        out_ref[:, j * 128 : (j + 1) * 128] = v.T
    for cp in pending:
        cp.wait_send()
    for stage in range(3):
        for k in range(3):
            for d in (1, 2, 3):
                row_copy(stage, k, d).wait_send()


def tail(hess, solved_t, coupling):
    tile = (8, 128)
    vm = lambda *lead: pltpu.VMEM(lead + tile, F32)
    sem = lambda n: pltpu.SemaphoreType.DMA((n,))
    vspec = pl.BlockSpec(memory_space=pltpu.VMEM)
    return pl.pallas_call(
        tail_kernel,
        in_specs=[vspec, vspec, pl.BlockSpec(memory_space=pl.ANY)],
        out_specs=vspec,
        out_shape=jax.ShapeDtypeStruct((128, 512), F32),
        scratch_shapes=[pltpu.VMEM((8, NB, 512), jnp.bfloat16)]
        + [vm(2, 4, 4, 4, n) for n in MAIN_N]
        + [vm(4, 4, 4, n) for n in MAIN_N]
        + [vm(3, 4, 4, n) for n in MAIN_N]
        + [vm(3, 4, n) for n in MAIN_N]
        + [
            vm(3, 16), vm(4, 16), pltpu.VMEM((512, 512), F32),
            vm(2, 80), vm(80), vm(80), vm(3, 20), vm(3, 5), vm(3, 5), vm(2, 80),
            pltpu.VMEM((512, 512), F32), pltpu.VMEM((4, 128, 128), F32),
            pltpu.VMEM((512, 128), F32),
            sem(8), sem(24), sem(24), pltpu.SemaphoreType.DMA, pltpu.SemaphoreType.DMA,
            sem(27), sem(27), sem(27), sem(27), sem(22), sem(22),
        ],
        compiler_params=pltpu.CompilerParams(
            collective_id=0, has_side_effects=True, vmem_limit_bytes=56 << 20
        ),
    )(hess, solved_t, coupling)


def per_device(coupling, scen_kkt, active_rows, first_hess):
    solved_t = scenario_solve(active_rows, scen_kkt[0], coupling[0])
    return tail(first_hess.reshape(4, 128), solved_t, coupling[0])


def solution(mesh):
    placed = (
        P(("scen", "grp"), None, None),
        P(("scen", "grp"), None, None),
        P(("scen", "grp")),
        P(),
    )
    return jax.shard_map(
        per_device, mesh=mesh, in_specs=placed, out_specs=P("scen", None), check_vma=False
    )
```

```python
import jax
import jax.numpy as jnp
from jax import lax
from jax.experimental import pallas as pl
from jax.experimental.pallas import tpu as pltpu
from jax.sharding import PartitionSpec as P

PW = 256
NC = 4096
NB = 768
F32 = jnp.float32
MESH = pl.DeviceIdType.MESH

ORDERS = (("x", "y", "z"), ("y", "z", "x"), ("z", "x", "y"))
MAIN_N = (5, 5, 6)
MAIN_OFF = (0, 5, 10)
HOOKS = (2, 3)
TOP_N = (4, 4, 2)
TOP_OFF = (0, 64, 128)


def total(terms):
    while len(terms) > 1:
        terms = [terms[i] + terms[i + 1] if i + 1 < len(terms) else terms[i] for i in range(0, len(terms), 2)]
    return terms[0]

def pair_factor(e):
    inv, l, t = {}, {}, {}
    for c in range(0, 8, 2):
        d = c + 1
        a = e[c, c]
        b = e[d, c]
        ra = lax.rsqrt(a)
        rd = lax.rsqrt(a * e[d, d] - b * b)
        inv[c] = ra
        inv[d] = (a * ra) * rd
        l[d, c] = b * ra
        for r in range(c + 2, 8):
            l[r, c] = e[r, c] * ra
            l[r, d] = (e[r, d] - l[r, c] * l[d, c]) * inv[d]
        for r in range(c + 2, 8):
            for q in range(c + 2, r + 1):
                e[r, q] = (e[r, q] - l[r, c] * l[q, c]) - l[r, d] * l[q, d]
    return inv, l


def bc(x, r):
    return jnp.broadcast_to(x[r : r + 1, :], (8, 128))


def inverse_factor(z):
    shape = (8, 128)
    lane = lax.broadcasted_iota(jnp.int32, shape, 1)
    sub = lax.broadcasted_iota(jnp.int32, shape, 0)
    z = list(z)
    for j in range(16):
        lo = 8 * j
        zj = z[j]
        panel = (lane >= lo) & (lane < lo + 8)
        zp = jnp.where(panel, jnp.where(lane - lo == sub, 1.0, 0.0), zj)
        rows = [bc(zj, r) for r in range(8)]
        zero = jnp.zeros(shape, F32)
        e = {(r, c): jnp.broadcast_to((rows[r] + zero)[:, lo + c : lo + c + 1], shape) for c in range(8) for r in range(c, 8)}
        inv, l = pair_factor(e)
        t = {}
        for c in range(8):
            t[c, c] = inv[c]
            for r in range(c + 1, 8):
                t[r, c] = -inv[r] * total([l[r, m] * t[m, c] for m in range(c, r)])
        zb = [bc(zp, c) for c in range(8)]
        u = [total([t[r, c] * zb[c] for c in range(r + 1)]) for r in range(8)]
        w = [total([t[c, r] * u[c] for c in range(r, 8)]) for r in range(8)]
        row = u[0]
        for r in range(1, 8):
            row = jnp.where(sub == r, u[r], row)
        z[j] = jnp.where(lane < lo + 8, row, 0.0)
        for i in range(j + 1, 16):
            zi = z[i]
            q = [jnp.broadcast_to(zi[:, lo + c : lo + c + 1], shape) * w[c] for c in range(8)]
            z[i] = jnp.where(panel, 0.0, zi) - total(q)
    return z


BF16 = jnp.bfloat16

def halves(a):
    hi = a.astype(BF16)
    return hi, (a - hi.astype(F32)).astype(BF16)

def left(a, axis):
    hi, lo = halves(a)
    return jnp.concatenate([hi, lo, hi], axis)

def right(a):
    hi, lo = halves(a)
    return jnp.concatenate([hi, hi, lo], 0)

def dot(a, b):
    return jnp.dot(left(a, 1), right(b), preferred_element_type=F32)

def dot_t(a, b):
    return lax.dot_general(left(a, 0), right(b), (((0,), (0,)), ((), ())), preferred_element_type=F32)

UPPER = ((0, 0), (0, 1), (1, 1), (0, 2), (1, 2), (0, 3), (1, 3), (2, 2), (2, 3), (3, 3))


def step_kernel(
    act_ref, hess_ref, kkt_ref, coup_ref, out_ref,
    kbuf, big, blinv, xs, yl, yr, stop, st_ref, tinv, tl,
    cbuf, ma, mb, mc, ra, rb, rc, pa, pb, pc, qa, qb, qc, last_slots, own,
    top, tacc, ta, t0, t1, t2, gat, aug, linv,
    k_sem, c_sem, core_s, core_r, tcore_s, tcore_r, tback_s, tback_r, st_s, st_r, tst_s, tst_r, ag_s, ag_r,
):
    si = lax.axis_index("scen")
    gi = lax.axis_index("grp")
    c = gi % 2
    zh = gi // 2
    pos = {"y": si // 8, "x": (si // 2) % 4, "z": 2 * zh + si % 2}
    main, recv_core = (ma, mb, mc), (ra, rb, rc)
    slots = ((pa, pb, pc), (qa, qb, qc))

    kload = pltpu.make_async_copy(kkt_ref, kbuf, k_sem)
    kload.start()
    loads = [
        pltpu.make_async_copy(coup_ref.at[:, pl.ds(i * 512, 512)], cbuf.at[i], c_sem.at[i])
        for i in range(8)
    ]
    for cp in loads:
        cp.start()

    def device(y, x, z, core):
        return {"scen": (y * 4 + x) * 2 + z % 2, "grp": (z // 2) * 2 + core}

    def peer(axis, dist):
        at = dict(pos)
        at[axis] = (at[axis] + dist) % 4
        return device(at["y"], at["x"], at["z"], c)

    partner = device(pos["y"], pos["x"], pos["z"], 1 - c)
    far = device(pos["y"], pos["x"], (pos["z"] + 2) % 4, 1 - c)

    barrier = pltpu.get_barrier_semaphore()
    greet = [peer(a, d) for a in "xyz" for d in (1, 2, 3)] + [partner, far]
    for dev in greet:
        pl.semaphore_signal(barrier, inc=1, device_id=dev, device_id_type=MESH)

    def meet():
        pl.semaphore_wait(barrier, len(greet))

    pending = []

    def send(src, dst, ssem, rsem, dev):
        cp = pltpu.make_async_remote_copy(
            src_ref=src, dst_ref=dst, send_sem=ssem, recv_sem=rsem,
            device_id=dev, device_id_type=MESH,
        )
        cp.start()
        pending.append(cp)
        return cp

    chunk_flights = []

    def region(k, y, x0):
        at = {"x": pl.ds(x0, 2), "y": y, "z": pl.ds(0, 4)}
        return tuple(at[a] for a in ORDERS[k])

    def chunk(i):
        y, x0 = i // 2, (i % 2) * 2
        if i:
            loads[i].wait()
        res = jnp.dot(st_ref[...], cbuf[i], preferred_element_type=F32)
        for t in range(4):
            x, zl = x0 + t // 2, t % 2
            part = res[:, t * 128 : (t + 1) * 128]
            for q in range(4):
                at = {"x": x, "y": y, "z": 2 * (q // 2) + zl}
                for k in range(3):
                    n = MAIN_N[k]
                    lo = q * 128 + MAIN_OFF[k] * 8
                    i0, i1, i2 = (at[a] for a in ORDERS[k])
                    main[k][q % 2, i0, i1, i2] = part[lo : lo + 8 * n].reshape(n, 8, 128)

    def chunk_send(i):
        y, x0 = i // 2, (i % 2) * 2
        out = []
        for k in range(3):
            r = region(k, y, x0)
            out.append(
                send(main[k].at[(1 - c,) + r], recv_core[k].at[r],
                     core_s.at[i * 3 + k], core_r.at[i * 3 + k], partner)
            )
        chunk_flights.append(out)

    def chunk_add(i):
        y, x0 = i // 2, (i % 2) * 2
        for k in range(3):
            chunk_flights[i][k].wait_recv()
            r = region(k, y, x0)
            main[k][(c,) + r] = main[k][(c,) + r] + recv_core[k][r]

    def top_tiles():
        for i, (a, b) in enumerate(UPPER):
            v = stop[a * 128 : (a + 1) * 128, b * 128 : (b + 1) * 128]
            top[i * 16 : i * 16 + 16] = v.reshape(16, 8, 128)

    def add_top():
        for a in range(4):
            lo, hi = a * 128, a * 128 + 128
            stop[lo:hi, lo:] += lax.dot_general(
                yl[:, NB + lo : NB + hi], yr[:, NB + lo :], (((0,), (0,)), ((), ())),
                preferred_element_type=F32,
            )

    def forward(j, _):
        at = pl.multiple_of(j * 128, 128)
        rows = pl.ds(at, 128)
        z = [big[pl.ds(at + 8 * i, 8), pl.ds(at, 128)] for i in range(16)]
        add_top()
        z = inverse_factor(z)
        for i in range(16):
            blinv[j, 8 * i : 8 * i + 8, :] = z[i]
        y = dot(blinv[j], big[rows, :])
        big[rows, :] = y
        hi, lo = halves(y)
        yl[0:128] = hi
        yl[128:256] = lo
        yl[256:384] = hi
        yr[0:128] = hi
        yr[128:256] = hi
        yr[256:384] = lo

        def update(i, _):
            ai = pl.multiple_of(i * 128, 128)
            below = pl.ds(ai, 128)
            big[below, :] = big[below, :] - lax.dot_general(
                yl[:, pl.ds(ai, 128)], yr[...], (((0,), (0,)), ((), ())), preferred_element_type=F32
            )
            return 0

        lax.fori_loop(j + 1, NB // 128, update, 0)
        return 0

    def backward(*blocks):
        for j in blocks:
            lo, hi = j * 128, j * 128 + 128
            acc = big[lo:hi, NB:]
            if hi < NB:
                acc = acc - dot(big[lo:hi, hi:NB], xs[hi:, :])
            x = dot_t(blinv[j], acc)
            xs[lo:hi, :] = x
            st_ref[:, lo:hi] = (x * kept(lo, hi)).T.astype(BF16)

    def kept(lo, hi):
        row = lax.broadcasted_iota(jnp.int32, (hi - lo, 1), 0) + lo
        return (row < act_ref[0]).astype(F32)

    def remote(src, dst, ssem, rsem, dev):
        return pltpu.make_async_remote_copy(
            src_ref=src, dst_ref=dst, send_sem=ssem, recv_sem=rsem,
            device_id=dev, device_id_type=MESH,
        )

    def to_core_0():
        return remote(top, ta, tcore_s, tcore_r, partner)

    def to_core_1():
        return remote(gat, gat, tback_s, tback_r, partner)

    def top_base(k, stage):
        base = TOP_OFF[k]
        if stage >= 1:
            base = base + pos[ORDERS[k][0]] * (4 * TOP_N[k])
        if stage >= 2:
            base = base + pos[ORDERS[k][1]] * TOP_N[k]
        return base

    def top_copy(stage, k, d):
        axis = ORDERS[k][(0, 1, 2, 1, 0)[stage]]
        n = TOP_N[k] * (4 if stage in (0, 4) else 1)
        if stage < 2:
            src = tacc.at[pl.ds(top_base(k, stage) + (pos[axis] + d) % 4 * n, n)]
            dst = (t0, t1)[stage].at[d - 1, pl.ds(TOP_OFF[k] // (4, 16)[stage], n)]
        elif stage == 2:
            src = tacc.at[pl.ds(top_base(k, 2), n)]
            dst = t2.at[d - 1, pl.ds(TOP_OFF[k] // 16, n)]
        else:
            src = dst = gat.at[pl.ds(top_base(k, 5 - stage), n)]
        i = (stage * 3 + k) * 3 + d - 1
        return remote(src, dst, tst_s.at[i], tst_r.at[i], peer(axis, d))

    def top_start(stage):
        for k in range(3):
            for d in (1, 2, 3):
                top_copy(stage, k, d).start()

    def top_wait(stage):
        for k in range(3):
            for d in (1, 2, 3):
                top_copy(stage, k, d).wait_recv()

    def top_sum(stage):
        got = (t0, t1)[stage]
        top_wait(stage)
        for k in range(3):
            n = TOP_N[k] * (4, 1)[stage]
            mine, sl = pl.ds(top_base(k, stage + 1), n), pl.ds(TOP_OFF[k] // (4, 16)[stage], n)
            tacc[mine] = (tacc[mine] + got[0, sl]) + (got[1, sl] + got[2, sl])

    def top_total():
        top_wait(2)
        for k in range(3):
            n, off, mine = TOP_N[k], TOP_OFF[k] // 16, pos[ORDERS[k][2]]
            own_part = pl.ds(top_base(k, 2), n)
            parts = [tacc[own_part]] + [t2[d, pl.ds(off, n)] for d in range(3)]
            vals = []
            for p in range(4):
                dist = (mine - p) % 4
                vals.append(jnp.where(
                    dist == 0, parts[0],
                    jnp.where(dist == 1, parts[1], jnp.where(dist == 2, parts[2], parts[3])),
                ))
            gat[own_part] = (vals[0] + vals[1]) + (vals[2] + vals[3])

    def where(k, stage):
        return (c,) + tuple(pos[a] for a in ORDERS[k][:stage])

    def row_copy(stage, k, d):
        axis = ORDERS[k][stage]
        src = main[k].at[where(k, stage) + ((pos[axis] + d) % 4,)]
        dst = last_slots.at[d - 1, pl.ds(MAIN_OFF[k], MAIN_N[k])] if stage == 2 else slots[stage][k].at[d - 1]
        i = (stage * 3 + k) * 3 + d - 1
        return pltpu.make_async_remote_copy(
            src_ref=src, dst_ref=dst, send_sem=st_s.at[i], recv_sem=st_r.at[i],
            device_id=peer(axis, d), device_id_type=MESH,
        )

    def row_scatter(stage, k):
        for d in (1, 2, 3):
            row_copy(stage, k, d).start()

    def row_sum(stage, k):
        for d in (1, 2, 3):
            row_copy(stage, k, d).wait_recv()
        at = where(k, stage + 1)
        got = [
            last_slots[d, pl.ds(MAIN_OFF[k], MAIN_N[k])] if stage == 2 else slots[stage][k][d]
            for d in range(3)
        ]
        total_rows = (main[k][at] + got[0]) + (got[1] + got[2])
        if stage == 2:
            own[gi, pl.ds(MAIN_OFF[k], MAIN_N[k])] = total_rows
        else:
            main[k][at] = total_rows

    yl[...] = jnp.zeros_like(yl)
    yr[...] = jnp.zeros_like(yr)
    stop[...] = jnp.zeros_like(stop)
    kload.wait()
    big[:, :NB] = kbuf[...].astype(F32)
    loads[0].wait()
    big[:, NB:] = cbuf[0].astype(F32) * kept(0, NB)
    lax.fori_loop(0, NB // 128, forward, 0)
    add_top()
    top_tiles()
    meet()

    def product_and_core(*chunks):
        for i in chunks:
            chunk(i)
            chunk_send(i)

    first, second = c == 0, c == 1

    @pl.when(second)
    def _():
        to_core_0().start()

    backward(5)

    @pl.when(first)
    def _():
        to_core_0().wait_recv()
        tacc[...] = top[...] + ta[...]
        top_start(0)

    backward(4, 3, 2, 1)

    @pl.when(first)
    def _():
        top_sum(0)
        top_start(1)

    backward(0)
    product_and_core(0, 1, 2, 3)

    @pl.when(first)
    def _():
        top_sum(1)
        top_start(2)

    product_and_core(4, 5, 6, 7)

    @pl.when(first)
    def _():
        top_total()
        top_start(3)

    for i in range(8):
        chunk_add(i)

    @pl.when(second)
    def _():
        for k in range(3):
            row_scatter(0, k)
        to_core_1().wait_recv()

    @pl.when(first)
    def _():
        top_wait(3)
        top_start(4)
        for k in range(3):
            row_scatter(0, k)
        top_wait(4)
        to_core_1().start()

    row = lax.broadcasted_iota(jnp.int32, (128, 128), 0)
    lane = lax.broadcasted_iota(jnp.int32, (128, 128), 1)
    for i, (a, b) in enumerate(UPPER):
        v = gat[i * 16 : i * 16 + 16].reshape(128, 128)
        if a == b:
            v = v + jnp.where(row == lane, hess_ref[a : a + 1, :], 0.0)
        aug[a * 128 : (a + 1) * 128, b * 128 : (b + 1) * 128] = v

    def step(j, _):
        for stage, block in ((0, HOOKS[0]), (1, HOOKS[1])):
            @pl.when(j == block)
            def _():
                for k in range(3):
                    row_sum(stage, k)
                    row_scatter(stage + 1, k)

        at = pl.multiple_of(j * 128, 128)
        rows = pl.ds(at, 128)
        z = [aug[pl.ds(at + 8 * i, 8), pl.ds(at, 128)] for i in range(16)]
        z = inverse_factor(z)
        for i in range(16):
            linv[j, 8 * i : 8 * i + 8, :] = z[i]
        aug[rows, :] = dot(linv[j], aug[rows, :])

        def update(i, _):
            ai = pl.multiple_of(i * 128, 128)
            below = pl.ds(ai, 128)
            aug[below, :] = aug[below, :] - dot_t(aug[rows, pl.ds(ai, 128)], aug[rows, :])
            return 0

        lax.fori_loop(j + 1, 4, update, 0)
        return 0

    lax.fori_loop(0, 4, step, 0)

    for k in range(3):
        row_sum(2, k)

    mine = own.at[gi]
    flights = [
        send(mine, mine, ag_s.at[j], ag_r.at[j], dev)
        for j, dev in enumerate((partner, peer("z", 2), far))
    ]

    tinv[...] = jnp.zeros_like(tinv)
    for j in range(4):
        lo, hi = j * 128, j * 128 + 128
        if j:
            acc = dot_t(aug[:lo, lo:hi], tinv[:lo, :lo])
            tinv[lo:hi, :lo] = -dot(linv[j], acc)
        tinv[lo:hi, lo:hi] = linv[j]
    tl[...] = left(tinv[...], 1)

    for cp in flights:
        cp.wait_recv()

    sol = jnp.dot(tl[...], right(own[...].reshape(512, 128)), preferred_element_type=F32)
    at = pl.multiple_of(jnp.where(si < 4, si, 0) * 128, 128)
    for j in range(4):
        v = jnp.where(si < 4, aug[j * 128 : (j + 1) * 128, pl.ds(at, 128)], sol[j * 128 : (j + 1) * 128, :])
        v = jnp.where(j * 128 + row <= si * 128 + lane, v, 0.0)
        out_ref[:, j * 128 : (j + 1) * 128] = v.T
    for cp in pending:
        cp.wait_send()
    for stage in range(3):
        for k in range(3):
            for d in (1, 2, 3):
                row_copy(stage, k, d).wait_send()

    @pl.when(second)
    def _():
        to_core_0().wait_send()

    @pl.when(first)
    def _():
        to_core_1().wait_send()
        for stage in range(5):
            for k in range(3):
                for d in (1, 2, 3):
                    top_copy(stage, k, d).wait_send()


def whole_step(active, hess, kkt, coupling):
    tile = (8, 128)
    vm = lambda *lead: pltpu.VMEM(lead + tile, F32)
    sem = lambda n: pltpu.SemaphoreType.DMA((n,))
    vspec = pl.BlockSpec(memory_space=pltpu.VMEM)
    aspec = pl.BlockSpec(memory_space=pl.ANY)
    return pl.pallas_call(
        step_kernel,
        in_specs=[pl.BlockSpec(memory_space=pltpu.SMEM), vspec, aspec, aspec],
        out_specs=vspec,
        out_shape=jax.ShapeDtypeStruct((128, 512), F32),
        scratch_shapes=[
            pltpu.VMEM((NB, NB), BF16), pltpu.VMEM((NB, 1280), F32), pltpu.VMEM((6, 128, 128), F32),
            pltpu.VMEM((NB, 512), F32), pltpu.VMEM((384, 1280), BF16), pltpu.VMEM((384, 1280), BF16),
            pltpu.VMEM((512, 512), F32), pltpu.VMEM((512, NB), BF16), pltpu.VMEM((512, 512), F32),
            pltpu.VMEM((512, 1536), BF16), pltpu.VMEM((8, NB, 512), BF16),
        ]
        + [vm(2, 4, 4, 4, n) for n in MAIN_N]
        + [vm(4, 4, 4, n) for n in MAIN_N]
        + [vm(3, 4, 4, n) for n in MAIN_N]
        + [vm(3, 4, n) for n in MAIN_N]
        + [
            vm(3, 16), vm(4, 16),
            vm(160), vm(160), vm(160), vm(3, 40), vm(3, 10), vm(3, 10), vm(160),
            pltpu.VMEM((512, 512), F32), pltpu.VMEM((4, 128, 128), F32),
            pltpu.SemaphoreType.DMA, sem(8), sem(24), sem(24),
            pltpu.SemaphoreType.DMA, pltpu.SemaphoreType.DMA,
            pltpu.SemaphoreType.DMA, pltpu.SemaphoreType.DMA,
            sem(27), sem(27), sem(45), sem(45), sem(3), sem(3),
        ],
        compiler_params=pltpu.CompilerParams(
            collective_id=0, has_side_effects=True, vmem_limit_bytes=60 << 20
        ),
    )(active, hess, kkt, coupling)


def per_device(coupling, scen_kkt, active_rows, first_hess):
    return whole_step(active_rows, first_hess.reshape(4, 128), scen_kkt[0], coupling[0])


def solution(mesh):
    placed = (
        P(("scen", "grp"), None, None),
        P(("scen", "grp"), None, None),
        P(("scen", "grp")),
        P(),
    )
    return jax.shard_map(
        per_device, mesh=mesh, in_specs=placed, out_specs=P("scen", None), check_vma=False
    )
```
